32 devices in a mesh: ctx: 8 (over z, x), exp: 4 (over y, core).
Axes of the slice: x: 2, y: 2, z: 4, core: 2. Of those that a mesh axis runs over, the one named last changes fastest.
Arguments:
- attn_query: bfloat16 [8192, 2048], P('ctx', 'exp'), may hold values from -112 to 112
- attn_key: bfloat16 [8192, 2048], P('ctx', 'exp'), may hold values from -40 to 40
- attn_value: bfloat16 [8192, 2048], P('ctx', 'exp'), may hold values from -40 to 40
- prefix_state: float32 [8, 16, 128, 128], P('ctx', 'exp'), may hold values from -40960 to 40960
- moe_in: bfloat16 [8192, 2048], P(('ctx', 'exp')), may hold values from -6 to 6
- grad_out: bfloat16 [8192, 2048], P(('ctx', 'exp')), may hold values from -6 to 6
- router_gates: bfloat16 [8192, 1], P(('ctx', 'exp')), may hold values from 0.099609375 to 1
- expert_ids: int32 [8192, 1], P(('ctx', 'exp')), may hold values from 0 to 3; in each aligned block of 256 rows (0 to 255, 256 to 511, ...) at most 96 rows name the same one
- w_gate_up: bfloat16 [4, 2048, 1024], P('exp'), may hold values from -0.125 to 0.125
- w_down: bfloat16 [4, 512, 2048], P('exp'), may hold values from -0.25 to 0.25
- w_out: bfloat16 [2048, 2048], P('exp'), may hold values from -0.125 to 0.125
Outputs:
- grad_query: bfloat16 [8192, 2048], P('ctx', 'exp')
- grad_key: bfloat16 [8192, 2048], P('ctx', 'exp')
- grad_value: bfloat16 [8192, 2048], P('ctx', 'exp')
- grad_resid: bfloat16 [8192, 2048], P(('ctx', 'exp'))
- grad_gates: bfloat16 [8192, 1], P(('ctx', 'exp'))
- grad_gate_up: float32 [4, 2048, 1024], P('exp', 'ctx')
- grad_down: float32 [4, 512, 2048], P('exp', 'ctx')
The draws below stay inside these ranges and needn't reach their ends.
Inputs may be any that keep to these rules, and one draw needn't show every extreme that they name: `expert_ids`: among the 256 rows of one device (aligned blocks of rows) no expert is named more than 96 times, a bound that some block reaches.
All inputs are finite; a program needn't handle non-finite values.
Results may differ from the reference program's by a relative error of at most 0.0063.
Values may be sent and summed in bfloat16 or wider, within the bound.
A program may use at most 192 MiB of HBM per device.

```python
import math
import jax
import jax.numpy as jnp
import numpy as np
from jax import lax

D = 2048
FF = 512
HEADS = 16
HEAD_DIM = 128
TOPK = 1
ROWS = 256
FLIGHT = 4
TOK_CTX = 1024
TOKENS = 8192
BLOCKS = 8
CAP = 96


def levels(stream_key, extent, split, least, high):
    def one(axis_at, parts):
        heights = jax.random.uniform(jax.random.fold_in(jax.random.fold_in(stream_key, 6), axis_at), (parts,), jnp.float32, least / len(split), high / len(split))
        return jnp.repeat(jnp.exp(heights), extent[axis_at] // parts).reshape((-1,) + (1,) * (len(extent) - axis_at - 1))

    level = one(*split[0])
    for cut in split[1:]:
        level = level * one(*cut)
    return level


def assign_block(own_key, own, number, rows, amount, top, reach, slope):
    order = jax.random.permutation(own_key, amount)
    heavy_load, common = shares(amount, rows * top, reach, slope, True), shares(amount, rows * top, reach, slope, False)
    places = jnp.arange(amount)

    def named(lengths, turn):
        used = int((lengths > 0).sum())
        fixed = max(1, used // 4)
        passed = fixed + (places - fixed + turn * (used - fixed)) % max(1, amount - fixed)
        return jnp.zeros((amount,), jnp.int32).at[order[jnp.where(places < fixed, places, passed)]].set(jnp.asarray(lengths, jnp.int32))

    lengths = jnp.where(number % 4 == 0, named(heavy_load, number // 4), named(common, number - number // 4 - 1))
    mixed = jax.random.permutation(jax.random.fold_in(own, 3), amount)
    donor, receiver = mixed[0:amount // 2 * 2:2], mixed[1:amount // 2 * 2:2]
    margin = jnp.minimum(lengths[donor] - 1, reach - lengths[receiver]) // 2
    margin = jnp.where((donor == order[0]) | (receiver == order[0]) | (lengths[receiver] == 0), 0, jnp.maximum(margin, 0))
    passed = jax.random.randint(jax.random.fold_in(own, 4), (amount // 2,), 0, 1 << 20) % (margin + 1)
    lengths = lengths.at[donor].add(-passed).at[receiver].add(passed)
    members = jnp.searchsorted(jnp.cumsum(lengths), jnp.arange(rows * top), side="right").astype(jnp.int32)
    table = members.reshape(top, rows).T
    table = table[jax.random.permutation(jax.random.fold_in(own, 1), rows)]
    turn = jax.random.randint(jax.random.fold_in(own, 2), (rows, 1), 0, top)
    return jnp.take_along_axis(table, (jnp.arange(top)[None, :] + turn) % top, axis=1)


def shares(number_of, total, most, skew, full):
    loads = [(1 << 20) // math.isqrt(rank ** skew) + 1 for rank in range(1, number_of + 1)]
    largest = most if full else min(most, max(-(-total // number_of), total * loads[0] // sum(loads)))
    least = 1 if total - largest >= number_of - 1 else 0
    holding, rest = [largest] + [least] * (number_of - 1), total - largest - least * (number_of - 1)
    while rest > 0:
        movable = [i for i in range(1, number_of) if holding[i] < largest] or [i for i in range(1, number_of) if holding[i] < most]
        pool, remaining = sum([loads[i] for i in movable]), rest
        for i in movable:
            more = min(most - holding[i], max(1, remaining * loads[i] // pool), rest)
            holding[i] = holding[i] + more
            rest = rest - more
    return np.array(holding)


def scatter_about(key, shape, scale, bound, split=(), kind=jnp.bfloat16):
    values = scale * jax.random.normal(key, shape, jnp.float32)
    if split:
        values = values * levels(key, shape, split, -0.22, 0.18)
    return jnp.clip(values, -bound, bound).astype(kind)


def setup_inputs(seed: int = 0) -> dict:
    seeds = jax.random.split(jax.random.key(seed), 12)
    attn_query = scatter_about(seeds[0], (TOKENS, HEADS * HEAD_DIM), (0.1 * (4 * TOKENS) ** 0.5), 112.0, ((0, 8), (1, 4)))
    attn_key = scatter_about(seeds[1], (TOKENS, HEADS * HEAD_DIM), (0.5 * (4 * TOKENS) ** 0.25), 40.0, ((0, 8), (1, 4)))
    attn_value = scatter_about(seeds[2], (TOKENS, HEADS * HEAD_DIM), (0.5 * (4 * TOKENS) ** 0.25), 40.0, ((0, 8), (1, 4)))
    prefix_state = scatter_about(seeds[3], (BLOCKS, HEADS, HEAD_DIM, HEAD_DIM), (0.25 * (3 * TOKENS) ** 0.5 * (4 * TOKENS) ** 0.5), 40960.0, ((0, 8), (1, 4)), jnp.float32)
    moe_in = scatter_about(seeds[4], (TOKENS, D), 1.0, 6.0, ((0, 32),))
    grad_out = scatter_about(seeds[5], (TOKENS, D), 0.5, 6.0, ((0, 32),))
    router_gates = jnp.clip(0.099609375 + 0.9003906 * jax.random.uniform(seeds[6], (TOKENS, TOPK), jnp.float32) ** levels(seeds[6], (TOKENS, TOPK), ((0, 32),), -0.2, 0.2), 0.099609375, 1.0).astype(jnp.bfloat16)
    expert_ids_keys = jax.random.split(jax.random.fold_in(seeds[7], 1), TOKENS // ROWS)
    expert_ids_turns = jax.random.permutation(jax.random.fold_in(seeds[7], 3), TOKENS // ROWS)
    expert_ids = jax.vmap(lambda own, number: assign_block(jax.random.fold_in(seeds[7], 2), own, number, ROWS, FLIGHT, TOPK, CAP, 1))(expert_ids_keys, expert_ids_turns).reshape((TOKENS, TOPK))
    w_gate_up = scatter_about(seeds[8], (FLIGHT, D, 2 * FF), D ** -0.5, 0.125, ((0, 4),))
    w_down = scatter_about(seeds[9], (FLIGHT, FF, D), FF ** -0.5, 0.25, ((0, 4),))
    w_out = scatter_about(seeds[10], (HEADS * HEAD_DIM, D), (HEADS * HEAD_DIM) ** -0.5, 0.125, ((0, 4),))
    return dict(attn_query=attn_query, attn_key=attn_key, attn_value=attn_value, prefix_state=prefix_state, moe_in=moe_in, grad_out=grad_out, router_gates=router_gates, expert_ids=expert_ids, w_gate_up=w_gate_up, w_down=w_down, w_out=w_out)


highest = lax.Precision.HIGHEST


def silu_slope(value):
    logistic = jax.nn.sigmoid(value)
    return logistic * (1.0 + value * (1.0 - logistic))


def contract_rows(left, right):
    return lax.dot_general(left, right, (((0,), (0,)), ((), ())), preferred_element_type=jnp.float32)


def contract_cols(left, right):
    return lax.dot_general(left, right, (((1,), (1,)), ((), ())), preferred_element_type=jnp.float32)


def expert_backward(inputs, gate_vals, w_pair, w_back, hidden_units):
    width = w_back.shape[1]
    rows_in = inputs[:, :width]
    cotangent = inputs[:, width:]
    both = jnp.dot(rows_in, w_pair, preferred_element_type=jnp.float32)
    first = both[:, :hidden_units]
    second = both[:, hidden_units:]
    hidden = (jax.nn.silu(first) * second).astype(jnp.bfloat16)
    output = jnp.dot(hidden, w_back, preferred_element_type=jnp.float32)
    cot_wide = cotangent.astype(jnp.float32)
    grad_gate = jnp.sum(cot_wide * output, axis=1).astype(jnp.bfloat16)
    scaled = (gate_vals.astype(jnp.float32)[:, None] * cot_wide).astype(jnp.bfloat16)
    grad_hidden = contract_cols(scaled, w_back)
    grad_first = grad_hidden * second * silu_slope(first)
    grad_second = grad_hidden * jax.nn.silu(first)
    grad_both = jnp.concatenate([grad_first, grad_second], axis=1).astype(jnp.bfloat16)
    grad_rows = contract_cols(grad_both, w_pair).astype(jnp.bfloat16)
    return rows_in, hidden, scaled, grad_both, grad_rows, grad_gate


def block_state(query_rows, grad_rows, counts):
    query_wide = query_rows.astype(jnp.float32)
    grad_wide = grad_rows.astype(jnp.float32) / counts[:, None, None]
    return jnp.einsum("uhj,uhi->hji", query_wide, grad_wide, precision=highest)


def attend_block(query_rows, key_rows, value_rows, grad_rows, prior, later, counts):
    scale_col = counts[:, None, None]
    inverse = 1.0 / counts
    position = jnp.arange(counts.shape[0], dtype=jnp.int32)
    lower = (position[None, :] <= position[:, None]).astype(jnp.float32)
    upper = (position[None, :] >= position[:, None]).astype(jnp.float32) * inverse[None, :]
    mix_query = (jnp.einsum("thd,uhd->htu", grad_rows, value_rows, preferred_element_type=jnp.float32)
                 * lower).astype(jnp.bfloat16)
    grad_query = (jnp.einsum("htu,uhd->thd", mix_query, key_rows, preferred_element_type=jnp.float32)
                  + jnp.einsum("thi,hji->thj", grad_rows.astype(jnp.float32), prior, precision=highest)) / scale_col
    mix_key = (jnp.einsum("thd,uhd->htu", value_rows, grad_rows, preferred_element_type=jnp.float32)
               * upper).astype(jnp.bfloat16)
    grad_key = (jnp.einsum("htu,uhd->thd", mix_key, query_rows, preferred_element_type=jnp.float32)
                + jnp.einsum("thi,hji->thj", value_rows.astype(jnp.float32), later, precision=highest))
    mix_value = (jnp.einsum("thd,uhd->htu", key_rows, query_rows, preferred_element_type=jnp.float32)
                 * upper).astype(jnp.bfloat16)
    grad_value = (jnp.einsum("htu,uhd->thd", mix_value, grad_rows, preferred_element_type=jnp.float32)
                  + jnp.einsum("thj,hji->thi", key_rows.astype(jnp.float32), later, precision=highest))
    return grad_query, grad_key, grad_value


def reference(attn_query, attn_key, attn_value, prefix_state, moe_in, grad_out, router_gates, expert_ids, w_gate_up, w_down, w_out):
    pair_total = TOKENS * TOPK
    block_count = TOKENS // ROWS
    flat_ids = expert_ids.reshape(pair_total)
    member = (flat_ids[:, None] == jnp.arange(FLIGHT, dtype=jnp.int32)[None, :]).astype(jnp.int32)
    member = member.reshape(block_count, ROWS * TOPK, FLIGHT)
    earlier = jnp.cumsum(member, axis=1) - member
    slot_of = jnp.sum(earlier * member, axis=2).reshape(pair_total)
    block_of = jnp.arange(pair_total, dtype=jnp.int32) // (ROWS * TOPK)
    table = jnp.full((FLIGHT, block_count * CAP), pair_total, jnp.int32)
    table = table.at[flat_ids, block_of * CAP + slot_of].set(jnp.arange(pair_total, dtype=jnp.int32))
    flat_gates = router_gates.reshape(pair_total)

    def one_expert(inputs):
        listing, w_pair, w_back = inputs
        token_of = listing // TOPK
        rows_in = jnp.take(moe_in, token_of, axis=0, mode="fill", fill_value=0)
        cotangent = jnp.take(grad_out, token_of, axis=0, mode="fill", fill_value=0)
        gate_vals = jnp.take(flat_gates, listing, axis=0, mode="fill", fill_value=0)
        joined = jnp.concatenate([rows_in, cotangent], axis=1)
        rows_in, hidden, scaled, grad_both, grad_rows, grad_gate = expert_backward(joined, gate_vals, w_pair, w_back, FF)
        return grad_rows, grad_gate, contract_rows(rows_in, grad_both), contract_rows(hidden, scaled)

    grad_rows, grad_gate, grad_gate_up, grad_down = lax.map(one_expert, (table, w_gate_up, w_down))
    flat_table = table.reshape(-1)
    pair_rows = jnp.zeros((pair_total, D), jnp.float32).at[flat_table].set(
        grad_rows.reshape(-1, D).astype(jnp.float32), mode="drop")
    grad_resid = (grad_out.astype(jnp.float32) + pair_rows.reshape(TOKENS, TOPK, D).sum(axis=1)).astype(jnp.bfloat16)
    grad_gates = jnp.zeros((pair_total,), jnp.bfloat16).at[flat_table].set(
        grad_gate.reshape(-1), mode="drop").reshape(TOKENS, TOPK)
    attn_grad = contract_cols(grad_resid, w_out).astype(jnp.bfloat16)

    block_shape = (BLOCKS, TOK_CTX, HEADS, HEAD_DIM)
    block_ids = jnp.arange(BLOCKS, dtype=jnp.int32)

    def counts_of(block):
        return (3 * TOKENS + block * TOK_CTX + jnp.arange(TOK_CTX, dtype=jnp.int32) + 1).astype(jnp.float32)

    def state_of(inputs):
        query, grad, block = inputs
        return block_state(query, grad, counts_of(block))

    queries = attn_query.reshape(block_shape)
    keys_all = attn_key.reshape(block_shape)
    values_all = attn_value.reshape(block_shape)
    grads_all = attn_grad.reshape(block_shape)
    states = lax.map(state_of, (queries, grads_all, block_ids))
    totals = jnp.cumsum(states[::-1], axis=0)[::-1]
    later_all = jnp.concatenate([totals[1:], jnp.zeros_like(states[:1])], axis=0)

    def grads_of(inputs):
        query, key_rows, value_rows, grad, prior, later, block = inputs
        results = attend_block(query, key_rows, value_rows, grad, prior, later, counts_of(block))
        return tuple(result.reshape(TOK_CTX, HEADS * HEAD_DIM).astype(jnp.bfloat16) for result in results)

    grad_query, grad_key, grad_value = lax.map(
        grads_of, (queries, keys_all, values_all, grads_all, prefix_state, later_all, block_ids))
    flat_shape = (TOKENS, HEADS * HEAD_DIM)
    return (grad_query.reshape(flat_shape), grad_key.reshape(flat_shape), grad_value.reshape(flat_shape),
            grad_resid, grad_gates, grad_gate_up, grad_down)
```

```python
import functools

import jax
import jax.numpy as jnp
from jax import lax
from jax.experimental import pallas as pl
from jax.experimental.pallas import tpu as pltpu
from jax.sharding import PartitionSpec as P

LANES = 128
MESH = pl.DeviceIdType.MESH
BF16 = jnp.bfloat16
F32 = jnp.float32


def contract_rows(left, right):
    return lax.dot_general(left, right, (((0,), (0,)), ((), ())), preferred_element_type=F32)


def contract_cols(left, right):
    return lax.dot_general(left, right, (((1,), (1,)), ((), ())), preferred_element_type=F32)


def plain(left, right):
    return jnp.dot(left, right, preferred_element_type=F32)


def bit_of(value, bit):
    return lax.rem(lax.div(value, bit), 2)


def flipped(value, mask):
    found, bit = value, 1
    while bit <= mask:
        if mask & bit:
            found = found + bit - 2 * bit * bit_of(value, bit)
        bit *= 2
    return found


def at_least(value, bound, size):
    return lax.div(value - bound + size, size)


class Sends:
    def __init__(self):
        self.open = []

    def start(self, src, dst, send, recv, device, when=None):
        copy = pltpu.make_async_remote_copy(
            src_ref=src, dst_ref=dst, send_sem=send, recv_sem=recv, device_id=device, device_id_type=MESH
        )
        self.open.append((copy, when))
        if when is None:
            copy.start()
        else:
            pl.when(when)(copy.start)
        return copy

    def drain(self):
        for copy, when in self.open:
            if when is None:
                copy.wait_send()
            else:
                pl.when(when)(copy.wait_send)


def layer_kernel(
    groups,
    blocks,
    chunk,
    target_ref,
    gates_ref,
    moe_ref,
    cot_ref,
    pair_hbm,
    back_hbm,
    proj_hbm,
    query_hbm,
    key_hbm,
    value_hbm,
    prior_hbm,
    dquery_ref,
    dkey_ref,
    dvalue_ref,
    resid_ref,
    dgates_ref,
    up_ref,
    down_ref,
    pair_ref,
    back_ref,
    proj_ref,
    query_ref,
    key_ref,
    value_ref,
    prior_ref,
    load_sem,
    targets_ref,
    target_sem,
    packed_ref,
    came_ref,
    token_sem,
    scaled_ref,
    both_ref,
    rows_t_ref,
    hidden_t_ref,
    gate_out_ref,
    gate_in_ref,
    gate_sem,
    rows_ref,
    rows_sem,
    slots_ref,
    grad_ref,
    scaled_grad_ref,
    local_ref,
    later_ref,
    line_ref,
    state_out_ref,
    state_in_ref,
    state_sem,
    pair_up_out,
    pair_up_in,
    pair_down_out,
    pair_down_in,
    pair_sem,
    line_up_out,
    line_up_in,
    line_down_out,
    line_down_in,
    line_sem,
):
    me, block = lax.axis_index("exp"), lax.axis_index("ctx")
    side, place = lax.rem(block, 2), lax.div(block, 2)
    length = blocks // 2
    tokens_own, width = moe_ref.shape
    capacity = came_ref.shape[1]
    hidden_units = back_ref.shape[0]
    heads, head_dim = prior_ref.shape[:2]
    tokens = query_ref.shape[0]
    sends = Sends()

    loads = []
    for at, (src, dst) in enumerate(
        [
            (pair_hbm, pair_ref),
            (back_hbm, back_ref),
            (proj_hbm, proj_ref),
            (query_hbm, query_ref),
            (key_hbm, key_ref),
            (value_hbm, value_ref),
            (prior_hbm, prior_ref),
        ]
    ):
        loads.append(pltpu.make_async_copy(src, dst, load_sem.at[at]))
        loads[-1].start()

    barrier = pltpu.get_barrier_semaphore()
    peers = [{"exp": flipped(me, k)} for k in range(1, groups)]
    shifts = [1]
    while shifts[-1] < blocks // 2:
        shifts.append(2 * shifts[-1])
    for shift in shifts:
        peers += [{"ctx": lax.rem(block + shift, blocks)}, {"ctx": lax.rem(block + blocks - shift, blocks)}]
    for peer in peers:
        pl.semaphore_signal(barrier, inc=1, device_id=peer, device_id_type=MESH)
    pl.semaphore_wait(barrier, len(peers))

    def near(k):
        return {"exp": flipped(me, k)}

    own_target = target_ref[0:1, :]

    def placing(expert, targets):
        spots = lax.broadcasted_iota(jnp.int32, (capacity, tokens_own), 0) + expert * capacity
        return jnp.where(spots == targets, 1.0, 0.0).astype(BF16)

    token_copies, target_copies = {}, {}
    for k in (2, 3, 1, 0):
        chosen = placing(flipped(me, k), own_target)
        out = packed_ref.at[k - 1] if k else came_ref.at[0]
        out[:, :width] = plain(chosen, moe_ref[...]).astype(BF16)
        out[:, width : 2 * width] = plain(chosen, cot_ref[...]).astype(BF16)
        out[:, 2 * width :] = plain(chosen, gates_ref[...]).astype(BF16)
        if k:
            token_copies[k] = sends.start(out, came_ref.at[k], token_sem.at[0, k], token_sem.at[1, k], near(k))
    targets_ref[0] = target_ref[...]
    for k in range(1, groups):
        target_copies[k] = sends.start(
            target_ref, targets_ref.at[k], target_sem.at[0, k], target_sem.at[1, k], near(k)
        )

    gate_copies, row_copies, relay_copies = {}, {}, {}

    def expert(which, part, begin, piece):
        for k in which:
            if k:
                token_copies[k].wait_recv()
        size = len(which) * capacity
        inner = pl.ds(begin, size)
        rows_in = jnp.concatenate([came_ref[k, :, :width] for k in which], axis=0)
        cot = jnp.concatenate([came_ref[k, :, width : 2 * width] for k in which], axis=0).astype(F32)
        gate = jnp.concatenate([came_ref[k, :, 2 * width :] for k in which], axis=0)[:, :1].astype(F32)
        scaled = (gate * cot).astype(BF16)
        scaled_ref[part, inner, :] = scaled
        both = plain(rows_in, pair_ref[...])
        first, second = both[:, :hidden_units], both[:, hidden_units:]
        logistic = jax.nn.sigmoid(first)
        silu = first * logistic
        hidden = (silu * second).astype(BF16)
        grad_hidden = contract_cols(scaled, back_ref[...])
        slope = logistic * (1.0 + first * (1.0 - logistic))
        both_ref[part, inner, :hidden_units] = (grad_hidden * second * slope).astype(BF16)
        both_ref[part, inner, hidden_units:] = (grad_hidden * silu).astype(BF16)
        grad_rows = contract_cols(both_ref[part, inner, :], pair_ref[...]).astype(BF16)
        at = pl.ds(part * 2 * capacity + begin, size)
        rows_ref[0, at, :] = (cot + grad_rows.astype(F32)).astype(BF16)
        for partner in (2, 1):
            row_copies[partner, piece] = sends.start(
                rows_ref.at[0, at], rows_ref.at[partner, at],
                rows_sem.at[0, partner, piece], rows_sem.at[1, partner, piece], near(partner),
            )
        output = plain(hidden, back_ref[...])
        grad_gate = jnp.sum(cot * output, axis=1, keepdims=True)
        for spot, k in enumerate(which):
            one = jnp.broadcast_to(grad_gate[spot * capacity : (spot + 1) * capacity], (capacity, LANES))
            if k:
                gate_out_ref[k - 1] = one.astype(BF16)
                gate_copies[k] = sends.start(
                    gate_out_ref.at[k - 1], gate_in_ref.at[k], gate_sem.at[0, k], gate_sem.at[1, k], near(k)
                )
            else:
                gate_in_ref[0] = one.astype(BF16)
        return hidden

    loads[0].wait()
    loads[1].wait()
    hidden = expert((0, 1), 0, 0, 0)
    hidden_t_ref[0] = hidden.T
    rows_t_ref[0] = jnp.concatenate([came_ref[0, :, :width], came_ref[1, :, :width]], axis=0).T
    hidden_2 = expert((2,), 1, 0, 1)
    hidden_3 = expert((3,), 1, capacity, 2)
    hidden_t_ref[1] = jnp.concatenate([hidden_2, hidden_3], axis=0).T
    rows_t_ref[1] = jnp.concatenate([came_ref[2, :, :width], came_ref[3, :, :width]], axis=0).T

    unit, unit_down = width // blocks, hidden_units // blocks

    def up_part(which):
        at = pl.ds(pl.multiple_of(which * unit, unit), unit)
        return plain(rows_t_ref[0, at, :], both_ref[0]) + plain(rows_t_ref[1, at, :], both_ref[1])

    def down_part(which):
        at = pl.ds(pl.multiple_of(which * unit_down, unit_down), unit_down)
        return plain(hidden_t_ref[0, at, :], scaled_ref[0]) + plain(hidden_t_ref[1, at, :], scaled_ref[1])

    right_half = lax.div(place, max(length // 2, 1))
    fewer = place * (1 - right_half) + (length - 1 - place) * right_half

    def item(j):
        both_ways = at_least(2 * fewer, j + 1, 4 * length)
        step = both_ways * (j // 2) + (1 - both_ways) * (j - fewer)
        major = 1 - both_ways * (j % 2)
        rightward = major * (1 - right_half) + (1 - major) * right_half
        return rightward * (length - 1 - step) + (1 - rightward) * step, rightward

    items = [item(j) for j in range(length - 1)] + [(place, None)]
    partner = {"ctx": block + 1 - 2 * side}
    pair_copies = []
    for j, (home, _) in enumerate(items):
        pair_up_out[j] = up_part(2 * home + 1 - side).astype(BF16)
        one = sends.start(pair_up_out.at[j], pair_up_in.at[j], pair_sem.at[0, 0, j], pair_sem.at[1, 0, j], partner)
        pair_down_out[j] = down_part(2 * home + 1 - side).astype(BF16)
        two = sends.start(pair_down_out.at[j], pair_down_in.at[j], pair_sem.at[0, 1, j], pair_sem.at[1, 1, j], partner)
        pair_copies.append((one, two))

    has_left, has_right = at_least(place, 1, 2 * length), at_least(length - 1 - place, 1, 2 * length)

    def came_along(kind, slot, buffer):
        pltpu.make_async_remote_copy(
            src_ref=buffer.at[slot], dst_ref=buffer.at[slot], send_sem=line_sem.at[0, kind, 0],
            recv_sem=line_sem.at[1, kind, slot], device_id=partner, device_id_type=MESH,
        ).wait_recv()

    def line_item(j):
        home, rightward = items[j]
        parts = [
            (0, up_ref, up_part, pair_up_in, line_up_out, line_up_in),
            (1, down_ref, down_part, pair_down_in, line_down_out, line_down_in),
        ]
        for kind, total, part, pair_in, out, line_in in parts:
            pair_copies[j][kind].wait_recv()
            total[...] = part(2 * home + side) + pair_in[j].astype(F32)
            if rightward is None:
                ways = [(has_left, place + 1), (has_right, place)]
            else:
                ways = [(rightward * has_left + (1 - rightward) * has_right, home + rightward)]
            for present, slot in ways:

                @pl.when(present == 1)
                def _():
                    came_along(kind, slot, line_in)
                    total[...] += line_in[slot].astype(F32)

            if rightward is not None:
                out[j] = total[...].astype(BF16)
                sends.start(
                    out.at[j], line_in.at[home + rightward], line_sem.at[0, kind, j],
                    line_sem.at[1, kind, home + rightward], {"ctx": block + 4 * rightward - 2},
                )

    pieces = [pl.ds(0, 2 * capacity), pl.ds(2 * capacity, capacity), pl.ds(3 * capacity, capacity)]
    loads[2].wait()

    def project(j, piece):
        slots_ref[j, pieces[piece], :] = contract_cols(rows_ref[j, pieces[piece], :], proj_ref[...]).astype(BF16)

    def relay(piece):
        row_copies[2, piece].wait_recv()
        relay_copies[piece] = sends.start(
            rows_ref.at[2, pieces[piece]], rows_ref.at[3, pieces[piece]],
            rows_sem.at[0, 3, piece], rows_sem.at[1, 3, piece], near(1),
        )

    for piece in range(3):
        project(0, piece)
    for piece in range(3):
        row_copies[1, piece].wait_recv()
        project(1, piece)
    relay(0)
    project(2, 0)
    relay_copies[0].wait_recv()
    project(3, 0)
    line_item(0)
    relay(1)
    project(2, 1)
    relay_copies[1].wait_recv()
    project(3, 1)
    relay(2)
    project(2, 2)
    relay_copies[2].wait_recv()
    project(3, 2)

    base = (3 * blocks + block) * tokens
    for at in (3, 4, 5):
        loads[at].wait()

    def inverse_counts(start, shape):
        counts = base + start + 1 + lax.broadcasted_iota(jnp.int32, shape, 0)
        return 1.0 / counts.astype(F32)

    for i in range(groups):
        if i:
            target_copies[i].wait_recv()
        targets = targets_ref[i, 0:1, :]
        chosen = jnp.concatenate([placing(flipped(me, j), targets) for j in range(groups)], axis=0)
        found = jnp.concatenate(
            [slots_ref[j, (j ^ i) * capacity : ((j ^ i) + 1) * capacity, :] for j in range(groups)], axis=0
        )
        start = pl.multiple_of(flipped(me, i) * tokens_own, tokens_own)
        at = pl.ds(start, tokens_own)
        grads = contract_rows(chosen, found)
        scaled = (grads * inverse_counts(start, grads.shape)).astype(BF16)
        grad_ref[at, :] = grads.astype(BF16)
        scaled_grad_ref[at, :] = scaled
        for h in range(heads):
            cols = slice(h * head_dim, (h + 1) * head_dim)
            state = contract_rows(query_ref[at, cols], scaled[:, cols])
            local_ref[h] = state + local_ref[h] if i else state

    state_out_ref[0] = local_ref[...].astype(BF16)
    pair_state = sends.start(state_out_ref.at[0], state_in_ref.at[0], state_sem.at[0, 0], state_sem.at[1, 0], partner)

    own = jnp.concatenate([placing(flipped(me, j), own_target) for j in range(groups)], axis=0)
    rows = jnp.concatenate([rows_ref[j, j * capacity : (j + 1) * capacity, :] for j in range(groups)], axis=0)
    resid_ref[...] = contract_rows(own, rows).astype(BF16)
    for k in range(1, groups):
        gate_copies[k].wait_recv()
    gates = jnp.concatenate([gate_in_ref[k] for k in range(groups)], axis=0)
    dgates_ref[...] = contract_rows(own, gates)[:, :1].astype(BF16)

    pair_state.wait_recv()
    local_ref[...] = local_ref[...] + state_in_ref[0].astype(F32)
    later_ref[...] = state_in_ref[0].astype(F32) * (1 - side).astype(F32)
    line_ref[...] = jnp.zeros_like(line_ref)
    turn, step, steps = 1, 1, []
    while step < length:
        steps.append((turn, step))
        turn, step = turn + 1, 2 * step

    def send_state(turn, step):
        state_out_ref[turn] = (local_ref[...] + line_ref[...]).astype(BF16)
        sends.start(
            state_out_ref.at[turn], state_in_ref.at[turn], state_sem.at[0, turn], state_sem.at[1, turn],
            {"ctx": lax.rem(block + blocks - 2 * step, blocks)}, when=place >= step,
        )

    def take_state(turn, step):
        @pl.when(place + step < length)
        def _():
            pltpu.make_async_remote_copy(
                src_ref=state_in_ref.at[turn], dst_ref=state_in_ref.at[turn], send_sem=state_sem.at[0, turn],
                recv_sem=state_sem.at[1, turn], device_id=partner, device_id_type=MESH,
            ).wait_recv()
            line_ref[...] += state_in_ref[turn].astype(F32)

    row = lax.broadcasted_iota(jnp.int32, (chunk, chunk), 0)
    col = lax.broadcasted_iota(jnp.int32, (chunk, chunk), 1)

    def forward(h, carry):
        cols = pl.ds(pl.multiple_of(h * head_dim, head_dim), head_dim)
        state = prior_ref[h]
        for at in range(tokens // chunk):
            rows = pl.ds(at * chunk, chunk)
            keys, values, grads = key_ref[rows, cols], value_ref[rows, cols], grad_ref[rows, cols]
            mix = jnp.where(col <= row, contract_cols(grads, values), 0.0).astype(BF16)
            out = plain(mix, keys) + contract_cols(grads, state.astype(BF16))
            dquery_ref[rows, cols] = (out * inverse_counts(at * chunk, out.shape)).astype(BF16)
            state = state + contract_rows(keys, values)
        return carry

    def backward(h, carry):
        cols = pl.ds(pl.multiple_of(h * head_dim, head_dim), head_dim)
        state = later_ref[h] + line_ref[h]
        for at in reversed(range(tokens // chunk)):
            rows = pl.ds(at * chunk, chunk)
            query, keys = query_ref[rows, cols], key_ref[rows, cols]
            values, scaled = value_ref[rows, cols], scaled_grad_ref[rows, cols]
            held = state.astype(BF16)
            mix_key = jnp.where(col >= row, contract_cols(values, scaled), 0.0).astype(BF16)
            dkey_ref[rows, cols] = (plain(mix_key, query) + contract_cols(values, held)).astype(BF16)
            mix_value = jnp.where(col >= row, contract_cols(keys, query), 0.0).astype(BF16)
            dvalue_ref[rows, cols] = (plain(mix_value, scaled) + plain(keys, held)).astype(BF16)
            state = state + contract_rows(query, scaled)
        return carry

    loads[6].wait()
    for at, (turn, step) in enumerate(steps):
        send_state(turn, step)
        if at == 0:
            if length > 2:
                line_item(1)
            lax.fori_loop(0, heads, forward, 0)
        take_state(turn, step)
    lax.fori_loop(0, heads, backward, 0)
    for j in range(2, length):
        line_item(j)
    sends.drain()


def compute(
    attn_query, attn_key, attn_value, prefix_state, moe_in, grad_out, router_gates, expert_ids,
    w_gate_up, w_down, w_out,
):
    groups, blocks = lax.axis_size("exp"), lax.axis_size("ctx")
    rows, width = moe_in.shape
    capacity = 3 * rows // (2 * groups * w_gate_up.shape[0])
    flat_ids = expert_ids.reshape(rows)
    place = jnp.arange(rows, dtype=jnp.int32)
    same = (flat_ids[:, None] == flat_ids[None, :]) & (place[:, None] < place[None, :])
    target = flat_ids * capacity + jnp.sum(same.astype(jnp.int32), axis=0)
    target = jnp.broadcast_to(target[None, :], (8, rows))
    gates = jnp.broadcast_to(router_gates, (rows, LANES))
    hidden_units, wide = w_down.shape[1], w_gate_up.shape[2]
    unit, unit_down = width // blocks, hidden_units // blocks
    tokens, cols = attn_query.shape
    heads, head_dim = prefix_state.shape[1:3]
    length = blocks // 2
    turns = max(length.bit_length(), 1)
    whole = pl.BlockSpec(memory_space=pltpu.VMEM)
    away = pl.BlockSpec(memory_space=pl.ANY)
    flat = jax.ShapeDtypeStruct((tokens, cols), BF16)
    dma = pltpu.SemaphoreType.DMA
    vmem = pltpu.VMEM
    scratch = [
        vmem((width, wide), BF16), vmem((hidden_units, width), BF16), vmem((cols, width), BF16),
        vmem((tokens, cols), BF16), vmem((tokens, cols), BF16), vmem((tokens, cols), BF16),
        vmem((heads, head_dim, head_dim), F32), dma((7,)),
        vmem((groups, 8, rows), jnp.int32), dma((2, groups)),
        vmem((groups - 1, capacity, 2 * width + LANES), BF16),
        vmem((groups, capacity, 2 * width + LANES), BF16), dma((2, groups)),
        vmem((2, 2 * capacity, width), BF16), vmem((2, 2 * capacity, wide), BF16),
        vmem((2, width, 2 * capacity), BF16), vmem((2, hidden_units, 2 * capacity), BF16),
        vmem((groups - 1, capacity, LANES), BF16), vmem((groups, capacity, LANES), BF16), dma((2, groups)),
        vmem((groups, groups * capacity, width), BF16), dma((2, groups, 3)),
        vmem((groups, groups * capacity, cols), BF16),
        vmem((tokens, cols), BF16), vmem((tokens, cols), BF16),
        vmem((heads, head_dim, head_dim), F32), vmem((heads, head_dim, head_dim), F32),
        vmem((heads, head_dim, head_dim), F32),
        vmem((turns, heads, head_dim, head_dim), BF16), vmem((turns, heads, head_dim, head_dim), BF16),
        dma((2, turns)),
        vmem((length, unit, wide), BF16), vmem((length, unit, wide), BF16),
        vmem((length, unit_down, width), BF16), vmem((length, unit_down, width), BF16), dma((2, 2, length)),
        vmem((length - 1, unit, wide), BF16), vmem((length + 1, unit, wide), BF16),
        vmem((length - 1, unit_down, width), BF16), vmem((length + 1, unit_down, width), BF16),
        dma((2, 2, length + 1)),
    ]
    return pl.pallas_call(
        functools.partial(layer_kernel, groups, blocks, min(256, tokens)),
        in_specs=[whole] * 4 + [away] * 7,
        out_specs=[whole] * 7,
        out_shape=[
            flat, flat, flat, jax.ShapeDtypeStruct((rows, width), BF16), jax.ShapeDtypeStruct((rows, 1), BF16),
            jax.ShapeDtypeStruct((unit, wide), F32), jax.ShapeDtypeStruct((unit_down, width), F32),
        ],
        scratch_shapes=scratch,
        compiler_params=pltpu.CompilerParams(
            collective_id=0, has_side_effects=True, vmem_limit_bytes=67043328
        ),
        name="layer",
    )(
        target, gates, moe_in, grad_out, w_gate_up[0], w_down[0], w_out, attn_query, attn_key, attn_value,
        prefix_state[0],
    )


def on_device(*args):
    dquery, dkey, dvalue, resid, dgates, up, down = compute(*args)
    return dquery, dkey, dvalue, resid, dgates, up[None], down[None]


def solution(mesh):
    return jax.shard_map(
        on_device,
        mesh=mesh,
        in_specs=(
            P("ctx", "exp"),
            P("ctx", "exp"),
            P("ctx", "exp"),
            P("ctx", "exp", None, None),
            P(("ctx", "exp"), None),
            P(("ctx", "exp"), None),
            P(("ctx", "exp"), None),
            P(("ctx", "exp"), None),
            P("exp", None, None),
            P("exp", None, None),
            P("exp", None),
        ),
        out_specs=(
            P("ctx", "exp"),
            P("ctx", "exp"),
            P("ctx", "exp"),
            P(("ctx", "exp"), None),
            P(("ctx", "exp"), None),
            P("exp", "ctx", None),
            P("exp", "ctx", None),
        ),
        check_vma=False,
    )
```

```python
import functools

import jax
import jax.numpy as jnp
from jax import lax
from jax.experimental import pallas as pl
from jax.experimental.pallas import tpu as pltpu
from jax.sharding import PartitionSpec as P

LANES = 128
MESH = pl.DeviceIdType.MESH
BF16 = jnp.bfloat16
F32 = jnp.float32


def contract_rows(left, right):
    return lax.dot_general(left, right, (((0,), (0,)), ((), ())), preferred_element_type=F32)


def contract_cols(left, right):
    return lax.dot_general(left, right, (((1,), (1,)), ((), ())), preferred_element_type=F32)


def plain(left, right):
    return jnp.dot(left, right, preferred_element_type=F32)


def bit_of(value, bit):
    return lax.rem(lax.div(value, bit), 2)


def flipped(value, mask):
    found, bit = value, 1
    while bit <= mask:
        if mask & bit:
            found = found + bit - 2 * bit * bit_of(value, bit)
        bit *= 2
    return found


def at_least(value, bound, size):
    return lax.div(value - bound + size, size)


class Sends:
    def __init__(self):
        self.open = []

    def start(self, src, dst, send, recv, device, when=None):
        copy = pltpu.make_async_remote_copy(
            src_ref=src, dst_ref=dst, send_sem=send, recv_sem=recv, device_id=device, device_id_type=MESH
        )
        self.open.append((copy, when))
        if when is None:
            copy.start()
        else:
            pl.when(when)(copy.start)
        return copy

    def drain(self):
        for copy, when in self.open:
            if when is None:
                copy.wait_send()
            else:
                pl.when(when)(copy.wait_send)


def layer_kernel(groups, blocks, chunk, direct, *refs):
    (
        ids_ref, gates_ref, moe_ref, cot_ref, pair_hbm, back_hbm, proj_hbm, query_hbm, key_hbm, value_hbm, prior_hbm,
        dquery_hbm, dkey_hbm, dvalue_hbm, resid_hbm, dgates_ref, up_hbm, down_hbm,
        pair_ref, back_ref, proj_ref, query_ref, key_ref, value_ref, prior_ref, load_sem,
        dquery_ref, dkey_ref, dvalue_ref, resid_ref, up_ref, down_ref, store_sem,
        targets_ref, target_sem, packed_ref, came_ref, token_sem,
        scaled_ref, both_ref, hidden_t_ref, gate_out_ref, gate_in_ref, gate_sem,
        rows_ref, rows_sem, slots_ref, grad_ref, scaled_grad_ref,
        local_ref, later_ref, line_ref, state_out_ref, state_in_ref, state_sem,
        pair_down_out, pair_down_in, pair_sem,
        line_up_out, line_up_in, line_down_out, line_down_in, line_sem,
    ) = refs[:63]
    if direct:
        other_rows_ref, other_both_ref, other_sem = refs[63:]
    else:
        rows_t_ref, pair_up_out, pair_up_in = refs[63:]
    me, block = lax.axis_index("exp"), lax.axis_index("ctx")
    side, place = lax.rem(block, 2), lax.div(block, 2)
    length = blocks // 2
    tokens_own, width = moe_ref.shape
    capacity = came_ref.shape[1]
    hidden_units = back_ref.shape[0]
    heads, head_dim = prior_ref.shape[:2]
    tokens = query_ref.shape[0]
    unit, unit_down = width // blocks, hidden_units // blocks
    partner = {"ctx": block + 1 - 2 * side}
    sends = Sends()

    loads = []
    for at, (src, dst) in enumerate(
        [
            (pair_hbm, pair_ref), (back_hbm, back_ref), (proj_hbm, proj_ref), (query_hbm, query_ref),
            (key_hbm, key_ref), (value_hbm, value_ref), (prior_hbm, prior_ref),
        ]
    ):
        loads.append(pltpu.make_async_copy(src, dst, load_sem.at[at]))
        loads[-1].start()
    stores = []

    def store(src, dst):
        stores.append(pltpu.make_async_copy(src, dst, store_sem.at[len(stores)]))
        stores[-1].start()

    barrier = pltpu.get_barrier_semaphore()
    peers = [{"exp": flipped(me, k)} for k in range(1, groups)]
    shifts = [1]
    while shifts[-1] < blocks // 2:
        shifts.append(2 * shifts[-1])
    for shift in shifts:
        peers += [{"ctx": lax.rem(block + shift, blocks)}, {"ctx": lax.rem(block + blocks - shift, blocks)}]
    for peer in peers:
        pl.semaphore_signal(barrier, inc=1, device_id=peer, device_id_type=MESH)

    def near(k):
        return {"exp": flipped(me, k)}

    ids = ids_ref[...]
    experts = lax.broadcasted_iota(jnp.int32, (8, tokens_own), 0)
    member = jnp.where(experts == ids, 1.0, 0.0)
    earlier = jnp.where(
        lax.broadcasted_iota(jnp.int32, (tokens_own, tokens_own), 0)
        < lax.broadcasted_iota(jnp.int32, (tokens_own, tokens_own), 1), 1.0, 0.0,
    )
    slot = jnp.sum(plain(member.astype(BF16), earlier.astype(BF16)) * member, axis=0, keepdims=True)
    own_target = ids * capacity + slot.astype(jnp.int32)
    targets_ref[0] = jnp.broadcast_to(own_target, (8, tokens_own))
    gates_row = gates_ref[...].astype(F32)

    def placing(expert, targets):
        spots = lax.broadcasted_iota(jnp.int32, (capacity, tokens_own), 0) + expert * capacity
        return jnp.where(spots == targets, 1.0, 0.0)

    token_copies, target_copies = {}, {}
    for k in (2, 3, 1, 0):
        found = placing(flipped(me, k), own_target)
        chosen = found.astype(BF16)
        out = packed_ref.at[k - 1] if k else came_ref.at[0]
        out[:, :width] = plain(chosen, moe_ref[...]).astype(BF16)
        out[:, width : 2 * width] = plain(chosen, cot_ref[...]).astype(BF16)
        gate = jnp.sum(found * gates_row, axis=1, keepdims=True)
        out[:, 2 * width :] = jnp.broadcast_to(gate, (capacity, LANES)).astype(BF16)
        if k == 2:
            pl.semaphore_wait(barrier, len(peers))
        if k:
            token_copies[k] = [
                sends.start(
                    out.at[:, cols], came_ref.at[k, :, cols], token_sem.at[0, k, half], token_sem.at[1, k, half], near(k)
                )
                for half, cols in enumerate((pl.ds(0, width), pl.ds(width, width + LANES)))
            ]
    for k in range(1, groups):
        target_copies[k] = sends.start(
            targets_ref.at[0], targets_ref.at[k], target_sem.at[0, k], target_sem.at[1, k], near(k)
        )

    gate_copies, row_copies, relay_copies = {}, {}, {}
    other_copies = []

    def other(src, dst):
        at = len(other_copies)
        other_copies.append(sends.start(src, dst, other_sem.at[0, at], other_sem.at[1, at], partner))

    def expert(which, part, begin, piece):
        size = len(which) * capacity
        inner = pl.ds(begin, size)
        for spot, k in enumerate(which):
            if k:
                token_copies[k][0].wait_recv()
            if direct:
                for home in range(length):
                    cols = pl.ds(pl.multiple_of((2 * home + 1 - side) * unit, unit), unit)
                    spots = pl.ds(begin + spot * capacity, capacity)
                    other(came_ref.at[k, :, cols], other_rows_ref.at[part, spots, pl.ds(home * unit, unit)])
        rows_in = jnp.concatenate([came_ref[k, :, :width] for k in which], axis=0)
        both = plain(rows_in, pair_ref[...])
        first, second = both[:, :hidden_units], both[:, hidden_units:]
        logistic = jax.nn.sigmoid(first)
        silu = first * logistic
        hidden = (silu * second).astype(BF16)
        slope = logistic * (1.0 + first * (1.0 - logistic))
        for k in which:
            if k:
                token_copies[k][1].wait_recv()
        cot = jnp.concatenate([came_ref[k, :, width : 2 * width] for k in which], axis=0).astype(F32)
        gate = jnp.concatenate([came_ref[k, :, 2 * width :] for k in which], axis=0)[:, :1].astype(F32)
        scaled = (gate * cot).astype(BF16)
        scaled_ref[part, inner, :] = scaled
        grad_hidden = contract_cols(scaled, back_ref[...])
        both_ref[part, inner, :hidden_units] = (grad_hidden * second * slope).astype(BF16)
        both_ref[part, inner, hidden_units:] = (grad_hidden * silu).astype(BF16)
        if direct:
            other(both_ref.at[part, inner], other_both_ref.at[part, inner])
        grad_rows = contract_cols(both_ref[part, inner, :], pair_ref[...]).astype(BF16)
        at = pl.ds(part * 2 * capacity + begin, size)
        rows_ref[0, at, :] = (cot + grad_rows.astype(F32)).astype(BF16)
        for peer in (2, 1):
            row_copies[peer, piece] = sends.start(
                rows_ref.at[0, at], rows_ref.at[peer, at],
                rows_sem.at[0, peer, piece], rows_sem.at[1, peer, piece], near(peer),
            )
        output = plain(hidden, back_ref[...])
        grad_gate = jnp.sum(cot * output, axis=1, keepdims=True)
        for spot, k in enumerate(which):
            one = jnp.broadcast_to(grad_gate[spot * capacity : (spot + 1) * capacity], (capacity, LANES))
            if k:
                gate_out_ref[k - 1] = one.astype(BF16)
                gate_copies[k] = sends.start(
                    gate_out_ref.at[k - 1], gate_in_ref.at[k], gate_sem.at[0, k], gate_sem.at[1, k], near(k)
                )
            else:
                gate_in_ref[0] = one.astype(BF16)
        return hidden

    pieces = [pl.ds(0, 2 * capacity), pl.ds(2 * capacity, capacity), pl.ds(3 * capacity, capacity)]

    def project(j, piece):
        slots_ref[j, pieces[piece], :] = contract_cols(rows_ref[j, pieces[piece], :], proj_ref[...]).astype(BF16)

    def project_near(piece):
        project(0, piece)
        row_copies[1, piece].wait_recv()
        project(1, piece)

    def project_far(piece):
        row_copies[2, piece].wait_recv()
        relay_copies[piece] = sends.start(
            rows_ref.at[2, pieces[piece]], rows_ref.at[3, pieces[piece]],
            rows_sem.at[0, 3, piece], rows_sem.at[1, 3, piece], near(1),
        )
        project(2, piece)
        relay_copies[piece].wait_recv()
        project(3, piece)

    loads[0].wait()
    loads[1].wait()
    hidden_t_ref[0] = expert((0, 1), 0, 0, 0).T
    if not direct:
        rows_t_ref[0] = jnp.concatenate([came_ref[0, :, :width], came_ref[1, :, :width]], axis=0).T
    loads[2].wait()
    project_near(0)
    hidden_2 = expert((2,), 1, 0, 1)
    project_near(1)
    hidden_3 = expert((3,), 1, capacity, 2)
    hidden_t_ref[1] = jnp.concatenate([hidden_2, hidden_3], axis=0).T
    if not direct:
        rows_t_ref[1] = jnp.concatenate([came_ref[2, :, :width], came_ref[3, :, :width]], axis=0).T

    def up_rows(which):
        at = pl.ds(pl.multiple_of(which * unit, unit), unit)
        return plain(rows_t_ref[0, at, :], both_ref[0]) + plain(rows_t_ref[1, at, :], both_ref[1])

    def up_pair(j, home):
        if not direct:
            pair_copies[0, j].wait_recv()
            return up_rows(2 * home + side) + pair_up_in[j].astype(F32)
        cols = pl.ds(pl.multiple_of((2 * home + side) * unit, unit), unit)
        there = pl.ds(pl.multiple_of(home * unit, unit), unit)
        found = None
        for part in range(2):
            here = jnp.concatenate([came_ref[2 * part, :, cols], came_ref[2 * part + 1, :, cols]], axis=0)
            one = contract_rows(here, both_ref[part])
            one = one + contract_rows(other_rows_ref[part, :, there], other_both_ref[part])
            found = one if found is None else found + one
        return found

    def down_rows(which):
        at = pl.ds(pl.multiple_of(which * unit_down, unit_down), unit_down)
        return plain(hidden_t_ref[0, at, :], scaled_ref[0]) + plain(hidden_t_ref[1, at, :], scaled_ref[1])

    right_half = lax.div(place, max(length // 2, 1))
    fewer = place * (1 - right_half) + (length - 1 - place) * right_half

    def item(j):
        both_ways = at_least(2 * fewer, j + 1, 4 * length)
        step = both_ways * (j // 2) + (1 - both_ways) * (j - fewer)
        major = 1 - both_ways * (j % 2)
        rightward = major * (1 - right_half) + (1 - major) * right_half
        return rightward * (length - 1 - step) + (1 - rightward) * step, rightward

    items = [item(j) for j in range(length - 1)] + [(place, None)]
    pair_copies = {}

    def pair_sends():
        for j, (home, _) in enumerate(items):
            if not direct:
                pair_up_out[j] = up_rows(2 * home + 1 - side).astype(BF16)
                pair_copies[0, j] = sends.start(
                    pair_up_out.at[j], pair_up_in.at[j], pair_sem.at[0, 0, j], pair_sem.at[1, 0, j], partner
                )
            pair_down_out[j] = down_rows(2 * home + 1 - side).astype(BF16)
            pair_copies[1, j] = sends.start(
                pair_down_out.at[j], pair_down_in.at[j], pair_sem.at[0, 1, j], pair_sem.at[1, 1, j], partner
            )

    has_left, has_right = at_least(place, 1, 2 * length), at_least(length - 1 - place, 1, 2 * length)
    inside = has_left * has_right

    def line_copy(kind, j, slot, device):
        out, line_in = ((line_up_out, line_up_in), (line_down_out, line_down_in))[kind]
        return pltpu.make_async_remote_copy(
            src_ref=out.at[j], dst_ref=line_in.at[slot], send_sem=line_sem.at[0, kind, j],
            recv_sem=line_sem.at[1, kind, slot], device_id=device, device_id_type=MESH,
        )

    def line_item(kind, j):
        home, rightward = items[j]
        total, out, line_in = ((up_ref, line_up_out, line_up_in), (down_ref, line_down_out, line_down_in))[kind]
        if kind:
            pair_copies[1, j].wait_recv()
            total[...] = down_rows(2 * home + side) + pair_down_in[j].astype(F32)
        else:
            total[...] = up_pair(j, home)
        if rightward is None:
            ways = [(has_left, place + 1), (has_right, place)]
        else:
            ways = [(rightward * has_left + (1 - rightward) * has_right, home + rightward)]
        for present, slot in ways:

            @pl.when(present == 1)
            def _():
                line_copy(kind, 0, slot, partner).wait_recv()
                total[...] += line_in[slot].astype(F32)

        if rightward is not None:
            out[j] = total[...].astype(BF16)
            line_copy(kind, j, home + rightward, {"ctx": block + 4 * rightward - 2}).start()

    def ends(*which):
        @pl.when(inside == 0)
        def _():
            for kind, j in which:
                if j < length - 1:
                    line_item(kind, j)

    def middles(*which):
        @pl.when(inside == 1)
        def _():
            for kind, j in which:
                if j < length - 1:
                    line_item(kind, j)

    pair_sends()
    project_near(2)
    for copy in other_copies:
        copy.wait_recv()
    ends((0, 0), (0, 1))
    project_far(0)
    middles((0, 0))
    project_far(1)
    ends((1, 0))
    project_far(2)

    base = (3 * blocks + block) * tokens
    for at in (3, 4, 5):
        loads[at].wait()

    def inverse_counts(start, shape):
        counts = base + start + 1 + lax.broadcasted_iota(jnp.int32, shape, 0)
        return 1.0 / counts.astype(F32)

    for i in range(groups):
        if i:
            target_copies[i].wait_recv()
        targets = targets_ref[i, 0:1, :]
        chosen = jnp.concatenate([placing(flipped(me, j), targets).astype(BF16) for j in range(groups)], axis=0)
        found = jnp.concatenate(
            [slots_ref[j, (j ^ i) * capacity : ((j ^ i) + 1) * capacity, :] for j in range(groups)], axis=0
        )
        start = pl.multiple_of(flipped(me, i) * tokens_own, tokens_own)
        at = pl.ds(start, tokens_own)
        grads = contract_rows(chosen, found)
        scaled = (grads * inverse_counts(start, grads.shape)).astype(BF16)
        grad_ref[at, :] = grads.astype(BF16)
        scaled_grad_ref[at, :] = scaled
        for h in range(heads):
            cols = slice(h * head_dim, (h + 1) * head_dim)
            state = contract_rows(query_ref[at, cols], scaled[:, cols])
            local_ref[h] = state + local_ref[h] if i else state

    state_out_ref[0] = local_ref[...].astype(BF16)
    pair_state = sends.start(state_out_ref.at[0], state_in_ref.at[0], state_sem.at[0, 0], state_sem.at[1, 0], partner)
    middles((0, 1))

    own = jnp.concatenate([placing(flipped(me, j), own_target).astype(BF16) for j in range(groups)], axis=0)
    rows = jnp.concatenate([rows_ref[j, j * capacity : (j + 1) * capacity, :] for j in range(groups)], axis=0)
    resid_ref[...] = contract_rows(own, rows).astype(BF16)
    store(resid_ref, resid_hbm)
    for k in range(1, groups):
        gate_copies[k].wait_recv()
    gates = jnp.concatenate([gate_in_ref[k] for k in range(groups)], axis=0)
    dgates_ref[...] = contract_rows(gates, own)[0:1, :].astype(BF16)

    pair_state.wait_recv()
    local_ref[...] = local_ref[...] + state_in_ref[0].astype(F32)
    later_ref[...] = state_in_ref[0].astype(F32) * (1 - side).astype(F32)
    line_ref[...] = jnp.zeros_like(line_ref)
    turn, step, steps = 1, 1, []
    while step < length:
        steps.append((turn, step))
        turn, step = turn + 1, 2 * step

    def send_state(turn, step):
        state_out_ref[turn] = (local_ref[...] + line_ref[...]).astype(BF16)
        sends.start(
            state_out_ref.at[turn], state_in_ref.at[turn], state_sem.at[0, turn], state_sem.at[1, turn],
            {"ctx": lax.rem(block + blocks - 2 * step, blocks)}, when=place >= step,
        )

    def take_state(turn, step):
        @pl.when(place + step < length)
        def _():
            pltpu.make_async_remote_copy(
                src_ref=state_in_ref.at[turn], dst_ref=state_in_ref.at[turn], send_sem=state_sem.at[0, turn],
                recv_sem=state_sem.at[1, turn], device_id=partner, device_id_type=MESH,
            ).wait_recv()
            line_ref[...] += state_in_ref[turn].astype(F32)

    row = lax.broadcasted_iota(jnp.int32, (chunk, chunk), 0)
    col = lax.broadcasted_iota(jnp.int32, (chunk, chunk), 1)

    def forward(h, carry):
        cols = pl.ds(pl.multiple_of(h * head_dim, head_dim), head_dim)
        state = prior_ref[h]
        for at in range(tokens // chunk):
            rows = pl.ds(at * chunk, chunk)
            keys, values, grads = key_ref[rows, cols], value_ref[rows, cols], grad_ref[rows, cols]
            mix = jnp.where(col <= row, contract_cols(grads, values), 0.0).astype(BF16)
            out = plain(mix, keys) + contract_cols(grads, state.astype(BF16))
            dquery_ref[rows, cols] = (out * inverse_counts(at * chunk, out.shape)).astype(BF16)
            state = state + contract_rows(keys, values)
        return carry

    def backward(h, carry):
        cols = pl.ds(pl.multiple_of(h * head_dim, head_dim), head_dim)
        state = later_ref[h] + line_ref[h]
        for at in reversed(range(tokens // chunk)):
            rows = pl.ds(at * chunk, chunk)
            query, keys = query_ref[rows, cols], key_ref[rows, cols]
            values, scaled = value_ref[rows, cols], scaled_grad_ref[rows, cols]
            held = state.astype(BF16)
            mix_key = jnp.where(col >= row, contract_cols(values, scaled), 0.0).astype(BF16)
            dkey_ref[rows, cols] = (plain(mix_key, query) + contract_cols(values, held)).astype(BF16)
            mix_value = jnp.where(col >= row, contract_cols(keys, query), 0.0).astype(BF16)
            dvalue_ref[rows, cols] = (plain(mix_value, scaled) + plain(keys, held)).astype(BF16)
            state = state + contract_rows(query, scaled)
        return carry

    loads[6].wait()
    if steps:
        send_state(*steps[0])
    for j in range(2, length - 1):
        line_item(0, j)
    lax.fori_loop(0, heads, forward, 0)
    store(dquery_ref, dquery_hbm)
    for at, one in enumerate(steps):
        if at:
            send_state(*one)
            if at == 1:
                middles((1, 0))
                for j in range(1, length - 1):
                    line_item(1, j)
        take_state(*one)
    lax.fori_loop(0, heads, backward, 0)
    store(dkey_ref, dkey_hbm)
    store(dvalue_ref, dvalue_hbm)
    line_item(0, length - 1)
    store(up_ref, up_hbm)
    line_item(1, length - 1)
    store(down_ref, down_hbm)
    for copy in stores:
        copy.wait()
    for kind in range(2):
        for j in range(length - 1):
            line_copy(kind, j, 0, partner).wait_send()
    sends.drain()


def pass_kernel(*refs):
    half = len(refs) // 2
    for src, dst in zip(refs[:half], refs[half:]):
        dst[...] = src[...]


def pass_on(*arrays):
    steps = 4
    specs = [
        pl.BlockSpec(one.shape, lambda i: (0, 0))
        if one.shape[0] % (16 * steps)
        else pl.BlockSpec((one.shape[0] // steps, one.shape[1]), lambda i: (i, 0))
        for one in arrays
    ]
    return pl.pallas_call(
        pass_kernel,
        grid=(steps,),
        in_specs=specs,
        out_specs=specs,
        out_shape=[jax.ShapeDtypeStruct(one.shape, one.dtype) for one in arrays],
        name="pass_on",
    )(*arrays)


def compute(
    attn_query, attn_key, attn_value, prefix_state, moe_in, grad_out, router_gates, expert_ids,
    w_gate_up, w_down, w_out,
):
    groups, blocks = lax.axis_size("exp"), lax.axis_size("ctx")
    rows, width = moe_in.shape
    capacity = 3 * rows // (2 * groups * w_gate_up.shape[0])
    hidden_units, wide = w_down.shape[1], w_gate_up.shape[2]
    unit, unit_down = width // blocks, hidden_units // blocks
    tokens, cols = attn_query.shape
    heads, head_dim = prefix_state.shape[1:3]
    length = blocks // 2
    turns = max(length.bit_length(), 1)
    direct = unit % LANES == 0
    whole = pl.BlockSpec(memory_space=pltpu.VMEM)
    away = pl.BlockSpec(memory_space=pl.ANY)
    flat = jax.ShapeDtypeStruct((tokens, cols), BF16)
    dma = pltpu.SemaphoreType.DMA
    vmem = pltpu.VMEM
    state = vmem((heads, head_dim, head_dim), F32)
    flat_ref = vmem((tokens, cols), BF16)
    scratch = [
        vmem((width, wide), BF16), vmem((hidden_units, width), BF16), vmem((cols, width), BF16),
        flat_ref, flat_ref, flat_ref, state, dma((7,)),
        flat_ref, flat_ref, flat_ref, vmem((rows, width), BF16), vmem((unit, wide), F32),
        vmem((unit_down, width), F32), dma((6,)),
        vmem((groups, 8, rows), jnp.int32), dma((2, groups)),
        vmem((groups - 1, capacity, 2 * width + LANES), BF16),
        vmem((groups, capacity, 2 * width + LANES), BF16), dma((2, groups, 2)),
        vmem((2, 2 * capacity, width), BF16), vmem((2, 2 * capacity, wide), BF16),
        vmem((2, hidden_units, 2 * capacity), BF16),
        vmem((groups - 1, capacity, LANES), BF16), vmem((groups, capacity, LANES), BF16), dma((2, groups)),
        vmem((groups, groups * capacity, width), BF16), dma((2, groups, 3)),
        vmem((groups, groups * capacity, cols), BF16),
        flat_ref, flat_ref,
        state, state, state,
        vmem((turns, heads, head_dim, head_dim), BF16), vmem((turns, heads, head_dim, head_dim), BF16),
        dma((2, turns)),
        vmem((length, unit_down, width), BF16), vmem((length, unit_down, width), BF16), dma((2, 2, length)),
        vmem((length - 1, unit, wide), BF16), vmem((length + 1, unit, wide), BF16),
        vmem((length - 1, unit_down, width), BF16), vmem((length + 1, unit_down, width), BF16),
        dma((2, 2, length + 1)),
    ]
    if direct:
        scratch += [
            vmem((2, 2 * capacity, length * unit), BF16), vmem((2, 2 * capacity, wide), BF16),
            dma((2, groups * length + 3)),
        ]
    else:
        scratch += [
            vmem((2, width, 2 * capacity), BF16),
            vmem((length, unit, wide), BF16), vmem((length, unit, wide), BF16),
        ]
    found = pl.pallas_call(
        functools.partial(layer_kernel, groups, blocks, min(256, tokens), direct),
        in_specs=[whole] * 4 + [away] * 7,
        out_specs=[away] * 4 + [whole] + [away] * 2,
        out_shape=[
            flat, flat, flat, jax.ShapeDtypeStruct((rows, width), BF16), jax.ShapeDtypeStruct((1, rows), BF16),
            jax.ShapeDtypeStruct((unit, wide), F32), jax.ShapeDtypeStruct((unit_down, width), F32),
        ],
        scratch_shapes=scratch,
        compiler_params=pltpu.CompilerParams(
            collective_id=0, has_side_effects=True, vmem_limit_bytes=67043328
        ),
        name="layer",
    )(
        expert_ids.reshape(1, rows), router_gates.reshape(1, rows), moe_in, grad_out, w_gate_up[0], w_down[0], w_out,
        attn_query, attn_key, attn_value, prefix_state[0],
    )
    dquery, dkey, dvalue, resid, dgates, up, down = pass_on(*found)
    return dquery, dkey, dvalue, resid, dgates.reshape(rows, 1), up, down


def on_device(*args):
    dquery, dkey, dvalue, resid, dgates, up, down = compute(*args)
    return dquery, dkey, dvalue, resid, dgates, up[None], down[None]


def solution(mesh):
    return jax.shard_map(
        on_device,
        mesh=mesh,
        in_specs=(
            P("ctx", "exp"),
            P("ctx", "exp"),
            P("ctx", "exp"),
            P("ctx", "exp", None, None),
            P(("ctx", "exp"), None),
            P(("ctx", "exp"), None),
            P(("ctx", "exp"), None),
            P(("ctx", "exp"), None),
            P("exp", None, None),
            P("exp", None, None),
            P("exp", None),
        ),
        out_specs=(
            P("ctx", "exp"),
            P("ctx", "exp"),
            P("ctx", "exp"),
            P(("ctx", "exp"), None),
            P(("ctx", "exp"), None),
            P("exp", "ctx", None),
            P("exp", "ctx", None),
        ),
        check_vma=False,
    )
```

```python
import functools

import jax
import jax.numpy as jnp
from jax import lax
from jax.experimental import pallas as pl
from jax.experimental.pallas import tpu as pltpu
from jax.sharding import PartitionSpec as P

LANES = 128
MESH = pl.DeviceIdType.MESH
BF16 = jnp.bfloat16
F32 = jnp.float32


def contract_rows(left, right):
    return lax.dot_general(left, right, (((0,), (0,)), ((), ())), preferred_element_type=F32)


def contract_cols(left, right):
    return lax.dot_general(left, right, (((1,), (1,)), ((), ())), preferred_element_type=F32)


def plain(left, right):
    return jnp.dot(left, right, preferred_element_type=F32)


def bit_of(value, bit):
    return lax.rem(lax.div(value, bit), 2)


def flipped(value, mask):
    found, bit = value, 1
    while bit <= mask:
        if mask & bit:
            found = found + bit - 2 * bit * bit_of(value, bit)
        bit *= 2
    return found


def at_least(value, bound, size):
    return lax.div(value - bound + size, size)


class Sends:
    def __init__(self):
        self.open = []

    def start(self, src, dst, send, recv, device, when=None):
        copy = pltpu.make_async_remote_copy(
            src_ref=src, dst_ref=dst, send_sem=send, recv_sem=recv, device_id=device, device_id_type=MESH
        )
        self.open.append((copy, when))
        if when is None:
            copy.start()
        else:
            pl.when(when)(copy.start)
        return copy

    def drain(self):
        for copy, when in self.open:
            if when is None:
                copy.wait_send()
            else:
                pl.when(when)(copy.wait_send)


def layer_kernel(groups, blocks, chunk, direct, *refs):
    (
        ids_ref, gates_ref, moe_ref, cot_ref, pair_hbm, back_hbm, proj_hbm, query_hbm, key_hbm, value_hbm, prior_hbm,
        dquery_hbm, dkey_hbm, dvalue_hbm, resid_hbm, dgates_ref, up_hbm, down_hbm,
        pair_ref, back_ref, proj_ref, query_ref, key_ref, value_ref, prior_ref, load_sem,
        dquery_ref, dkey_ref, dvalue_ref, resid_ref, up_ref, down_ref, store_sem,
        targets_ref, target_sem, packed_ref, came_ref, gate_packed_ref, gate_came_ref, token_sem,
        scaled_ref, both_ref, hidden_t_ref, gate_out_ref, gate_in_ref, gate_sem,
        rows_ref, rows_sem, slots_ref, grad_ref, scaled_grad_ref,
        local_ref, line_ref, state_out_ref, state_in_ref, state_sem,
        pair_down_out, pair_down_in, pair_sem,
        line_up_out, line_up_in, line_down_out, line_down_in, line_sem,
    ) = refs[:64]
    if direct:
        other_rows_ref, other_both_ref, other_sem = refs[64:]
    else:
        rows_t_ref, pair_up_out, pair_up_in = refs[64:]
    me, block = lax.axis_index("exp"), lax.axis_index("ctx")
    side, place = lax.rem(block, 2), lax.div(block, 2)
    length = blocks // 2
    tokens_own, width = moe_ref.shape
    capacity = came_ref.shape[1]
    hidden_units = back_ref.shape[0]
    heads, head_dim = prior_ref.shape[:2]
    tokens = query_ref.shape[0]
    unit, unit_down = width // blocks, hidden_units // blocks
    partner = {"ctx": block + 1 - 2 * side}
    sends = Sends()

    loads = []
    for at, (src, dst) in enumerate(
        [
            (pair_hbm, pair_ref), (back_hbm, back_ref), (proj_hbm, proj_ref), (query_hbm, query_ref),
            (key_hbm, key_ref), (value_hbm, value_ref), (prior_hbm, prior_ref),
        ]
    ):
        loads.append(pltpu.make_async_copy(src, dst, load_sem.at[at]))
        loads[-1].start()
    stores = []

    def store(src, dst):
        stores.append(pltpu.make_async_copy(src, dst, store_sem.at[len(stores)]))
        stores[-1].start()

    barrier = pltpu.get_barrier_semaphore()
    peers = [{"exp": flipped(me, k)} for k in range(1, groups)]
    shifts = [1]
    while shifts[-1] < blocks // 2:
        shifts.append(2 * shifts[-1])
    for shift in shifts:
        peers += [{"ctx": lax.rem(block + shift, blocks)}, {"ctx": lax.rem(block + blocks - shift, blocks)}]
    for peer in peers:
        pl.semaphore_signal(barrier, inc=1, device_id=peer, device_id_type=MESH)

    def near(k):
        return {"exp": flipped(me, k)}

    ids = ids_ref[...]
    experts = lax.broadcasted_iota(jnp.int32, (8, tokens_own), 0)
    member = jnp.where(experts == ids, 1.0, 0.0)
    earlier = jnp.where(
        lax.broadcasted_iota(jnp.int32, (tokens_own, tokens_own), 0)
        < lax.broadcasted_iota(jnp.int32, (tokens_own, tokens_own), 1), 1.0, 0.0,
    )
    slot = jnp.sum(plain(member.astype(BF16), earlier.astype(BF16)) * member, axis=0, keepdims=True)
    own_target = ids * capacity + slot.astype(jnp.int32)
    targets_ref[0] = jnp.broadcast_to(own_target, (8, tokens_own))
    gates_row = gates_ref[...].astype(F32)

    def placing(expert, targets):
        spots = lax.broadcasted_iota(jnp.int32, (capacity, tokens_own), 0) + expert * capacity
        return jnp.where(spots == targets, 1.0, 0.0)

    eye = jnp.where(
        lax.broadcasted_iota(jnp.int32, (capacity, LANES), 0) == lax.broadcasted_iota(jnp.int32, (capacity, LANES), 1),
        1.0, 0.0,
    )

    def as_row(column):
        return jnp.broadcast_to(jnp.sum(eye * column, axis=0, keepdims=True), (16, LANES)).astype(BF16)

    def as_column(rows):
        return jnp.sum(eye * rows[0:1, :].astype(F32), axis=1, keepdims=True)

    token_copies, target_copies = {}, {}
    for k in (2, 3, 1, 0):
        found = placing(flipped(me, k), own_target)
        chosen = found.astype(BF16)
        out = packed_ref.at[k - 1] if k else came_ref.at[0]
        out[:, :width] = plain(chosen, moe_ref[...]).astype(BF16)
        out[:, width : 2 * width] = plain(chosen, cot_ref[...]).astype(BF16)
        gate_out = gate_packed_ref.at[k - 1] if k else gate_came_ref.at[0]
        gate_out[...] = as_row(jnp.sum(found * gates_row, axis=1, keepdims=True))
        if k == 2:
            pl.semaphore_wait(barrier, len(peers))
        if k:
            token_copies[k] = [
                sends.start(
                    out.at[:, cols], came_ref.at[k, :, cols], token_sem.at[0, k, half], token_sem.at[1, k, half], near(k)
                )
                for half, cols in enumerate((pl.ds(0, width), pl.ds(width, width)))
            ]
            token_copies[k].append(
                sends.start(gate_out, gate_came_ref.at[k], token_sem.at[0, k, 2], token_sem.at[1, k, 2], near(k))
            )
    for k in range(1, groups):
        target_copies[k] = sends.start(
            targets_ref.at[0], targets_ref.at[k], target_sem.at[0, k], target_sem.at[1, k], near(k)
        )

    gate_copies, row_copies, relay_copies = {}, {}, {}
    other_copies = []

    def other(src, dst):
        at = len(other_copies)
        other_copies.append(sends.start(src, dst, other_sem.at[0, at], other_sem.at[1, at], partner))

    def expert(which, part, begin, piece):
        size = len(which) * capacity
        inner = pl.ds(begin, size)
        for spot, k in enumerate(which):
            if k:
                token_copies[k][0].wait_recv()
            if direct:
                for home in range(length):
                    cols = pl.ds(pl.multiple_of((2 * home + 1 - side) * unit, unit), unit)
                    spots = pl.ds(begin + spot * capacity, capacity)
                    other(came_ref.at[k, :, cols], other_rows_ref.at[part, spots, pl.ds(home * unit, unit)])
        rows_in = jnp.concatenate([came_ref[k, :, :width] for k in which], axis=0)
        both = plain(rows_in, pair_ref[...])
        first, second = both[:, :hidden_units], both[:, hidden_units:]
        logistic = jax.nn.sigmoid(first)
        silu = first * logistic
        hidden = (silu * second).astype(BF16)
        slope = logistic * (1.0 + first * (1.0 - logistic))
        for k in which:
            if k:
                token_copies[k][1].wait_recv()
                token_copies[k][2].wait_recv()
        cot = jnp.concatenate([came_ref[k, :, width : 2 * width] for k in which], axis=0).astype(F32)
        gate = jnp.concatenate([as_column(gate_came_ref[k]) for k in which], axis=0)
        scaled = (gate * cot).astype(BF16)
        scaled_ref[part, inner, :] = scaled
        grad_hidden = contract_cols(scaled, back_ref[...])
        both_ref[part, inner, :hidden_units] = (grad_hidden * second * slope).astype(BF16)
        both_ref[part, inner, hidden_units:] = (grad_hidden * silu).astype(BF16)
        if direct:
            other(both_ref.at[part, inner], other_both_ref.at[part, inner])
        grad_rows = contract_cols(both_ref[part, inner, :], pair_ref[...]).astype(BF16)
        at = pl.ds(part * 2 * capacity + begin, size)
        rows_ref[0, at, :] = (cot + grad_rows.astype(F32)).astype(BF16)
        for peer in (2, 1):
            row_copies[peer, piece] = sends.start(
                rows_ref.at[0, at], rows_ref.at[peer, at],
                rows_sem.at[0, peer, piece], rows_sem.at[1, peer, piece], near(peer),
            )
        output = plain(hidden, back_ref[...])
        grad_gate = jnp.sum(cot * output, axis=1, keepdims=True)
        for spot, k in enumerate(which):
            one = as_row(grad_gate[spot * capacity : (spot + 1) * capacity])
            if k:
                gate_out_ref[k - 1] = one
                gate_copies[k] = sends.start(
                    gate_out_ref.at[k - 1], gate_in_ref.at[k], gate_sem.at[0, k], gate_sem.at[1, k], near(k)
                )
            else:
                gate_in_ref[0] = one
        return hidden

    pieces = [pl.ds(0, 2 * capacity), pl.ds(2 * capacity, capacity), pl.ds(3 * capacity, capacity)]

    def project(j, piece):
        slots_ref[j, pieces[piece], :] = contract_cols(rows_ref[j, pieces[piece], :], proj_ref[...]).astype(BF16)

    def project_near(piece):
        project(0, piece)
        row_copies[1, piece].wait_recv()
        project(1, piece)

    def project_far(piece):
        row_copies[2, piece].wait_recv()
        relay_copies[piece] = sends.start(
            rows_ref.at[2, pieces[piece]], rows_ref.at[3, pieces[piece]],
            rows_sem.at[0, 3, piece], rows_sem.at[1, 3, piece], near(1),
        )
        project(2, piece)
        relay_copies[piece].wait_recv()
        project(3, piece)

    loads[0].wait()
    loads[1].wait()
    hidden_t_ref[0] = expert((0, 1), 0, 0, 0).T
    if not direct:
        rows_t_ref[0] = jnp.concatenate([came_ref[0, :, :width], came_ref[1, :, :width]], axis=0).T
    loads[2].wait()
    project_near(0)
    hidden_2 = expert((2,), 1, 0, 1)
    project_near(1)
    hidden_3 = expert((3,), 1, capacity, 2)
    hidden_t_ref[1] = jnp.concatenate([hidden_2, hidden_3], axis=0).T
    if not direct:
        rows_t_ref[1] = jnp.concatenate([came_ref[2, :, :width], came_ref[3, :, :width]], axis=0).T

    def up_rows(which):
        at = pl.ds(pl.multiple_of(which * unit, unit), unit)
        return plain(rows_t_ref[0, at, :], both_ref[0]) + plain(rows_t_ref[1, at, :], both_ref[1])

    def up_pair(j, home):
        if not direct:
            pair_copies[0, j].wait_recv()
            return up_rows(2 * home + side) + pair_up_in[j].astype(F32)
        cols = pl.ds(pl.multiple_of((2 * home + side) * unit, unit), unit)
        there = pl.ds(pl.multiple_of(home * unit, unit), unit)
        found = None
        for part in range(2):
            here = jnp.concatenate([came_ref[2 * part, :, cols], came_ref[2 * part + 1, :, cols]], axis=0)
            one = contract_rows(here, both_ref[part])
            one = one + contract_rows(other_rows_ref[part, :, there], other_both_ref[part])
            found = one if found is None else found + one
        return found

    def down_rows(which):
        at = pl.ds(pl.multiple_of(which * unit_down, unit_down), unit_down)
        return plain(hidden_t_ref[0, at, :], scaled_ref[0]) + plain(hidden_t_ref[1, at, :], scaled_ref[1])

    right_half = lax.div(place, max(length // 2, 1))
    fewer = place * (1 - right_half) + (length - 1 - place) * right_half

    def item(j):
        both_ways = at_least(2 * fewer, j + 1, 4 * length)
        step = both_ways * (j // 2) + (1 - both_ways) * (j - fewer)
        major = 1 - both_ways * (j % 2)
        rightward = major * (1 - right_half) + (1 - major) * right_half
        return rightward * (length - 1 - step) + (1 - rightward) * step, rightward

    items = [item(j) for j in range(length - 1)] + [(place, None)]
    pair_copies = {}

    def pair_sends():
        for j, (home, _) in enumerate(items):
            if not direct:
                pair_up_out[j] = up_rows(2 * home + 1 - side).astype(BF16)
                pair_copies[0, j] = sends.start(
                    pair_up_out.at[j], pair_up_in.at[j], pair_sem.at[0, 0, j], pair_sem.at[1, 0, j], partner
                )
            pair_down_out[j] = down_rows(2 * home + 1 - side).astype(BF16)
            pair_copies[1, j] = sends.start(
                pair_down_out.at[j], pair_down_in.at[j], pair_sem.at[0, 1, j], pair_sem.at[1, 1, j], partner
            )

    has_left, has_right = at_least(place, 1, 2 * length), at_least(length - 1 - place, 1, 2 * length)
    inside = has_left * has_right

    def line_copy(kind, j, slot, device):
        out, line_in = ((line_up_out, line_up_in), (line_down_out, line_down_in))[kind]
        return pltpu.make_async_remote_copy(
            src_ref=out.at[j], dst_ref=line_in.at[slot], send_sem=line_sem.at[0, kind, j],
            recv_sem=line_sem.at[1, kind, slot], device_id=device, device_id_type=MESH,
        )

    def line_item(kind, j):
        home, rightward = items[j]
        total, out, line_in = ((up_ref, line_up_out, line_up_in), (down_ref, line_down_out, line_down_in))[kind]
        if kind:
            pair_copies[1, j].wait_recv()
            total[...] = down_rows(2 * home + side) + pair_down_in[j].astype(F32)
        else:
            total[...] = up_pair(j, home)
        if rightward is None:
            ways = [(has_left, place + 1), (has_right, place)]
        else:
            ways = [(rightward * has_left + (1 - rightward) * has_right, home + rightward)]
        for present, slot in ways:

            @pl.when(present == 1)
            def _():
                line_copy(kind, 0, slot, partner).wait_recv()
                total[...] += line_in[slot].astype(F32)

        if rightward is not None:
            out[j] = total[...].astype(BF16)
            line_copy(kind, j, home + rightward, {"ctx": block + 4 * rightward - 2}).start()

    def ends(*which):
        @pl.when(inside == 0)
        def _():
            for kind, j in which:
                if j < length - 1:
                    line_item(kind, j)

    def middles(*which):
        @pl.when(inside == 1)
        def _():
            for kind, j in which:
                if j < length - 1:
                    line_item(kind, j)

    pair_sends()
    project_near(2)
    for copy in other_copies:
        copy.wait_recv()
    ends((0, 0), (1, 0), (0, 1), (1, 1))
    project_far(0)
    middles((0, 0))
    project_far(1)
    middles((1, 0))
    project_far(2)

    base = (3 * blocks + block) * tokens
    for at in (3, 4, 5):
        loads[at].wait()

    def inverse_counts(start, shape):
        counts = base + start + 1 + lax.broadcasted_iota(jnp.int32, shape, 0)
        return 1.0 / counts.astype(F32)

    for i in range(groups):
        if i:
            target_copies[i].wait_recv()
        targets = targets_ref[i, 0:1, :]
        chosen = jnp.concatenate([placing(flipped(me, j), targets).astype(BF16) for j in range(groups)], axis=0)
        found = jnp.concatenate(
            [slots_ref[j, (j ^ i) * capacity : ((j ^ i) + 1) * capacity, :] for j in range(groups)], axis=0
        )
        start = pl.multiple_of(flipped(me, i) * tokens_own, tokens_own)
        at = pl.ds(start, tokens_own)
        grads = contract_rows(chosen, found)
        scaled = (grads * inverse_counts(start, grads.shape)).astype(BF16)
        grad_ref[at, :] = grads.astype(BF16)
        scaled_grad_ref[at, :] = scaled
        for h in range(heads):
            cols = slice(h * head_dim, (h + 1) * head_dim)
            state = contract_rows(query_ref[at, cols], scaled[:, cols])
            local_ref[h] = state + local_ref[h] if i else state

    steps, step = [], 1
    while step < length:
        steps.append(step)
        step *= 2

    def state_copy(turn, device):
        return pltpu.make_async_remote_copy(
            src_ref=state_out_ref.at[turn], dst_ref=state_in_ref.at[turn], send_sem=state_sem.at[0, turn],
            recv_sem=state_sem.at[1, turn], device_id=device, device_id_type=MESH,
        )

    last = at_least(place, length - 1, 2 * length)

    def send_state(turn, chosen):
        @pl.when((place >= steps[turn]) & (chosen == 1))
        def _():
            value = local_ref[...] + line_ref[...] if turn else local_ref[...]
            state_out_ref[turn] = value.astype(BF16)
            state_copy(turn, {"ctx": lax.rem(block + blocks - 2 * steps[turn], blocks)}).start()

    def take_state(turn):
        @pl.when(place + steps[turn] < length)
        def _():
            state_copy(turn, partner).wait_recv()
            line_ref[...] += state_in_ref[turn].astype(F32)

    line_ref[...] = jnp.zeros_like(line_ref)
    if steps:
        send_state(0, 1)
    for turn in range(1, len(steps)):
        send_state(turn, last)
    for j in range(2, length - 1):
        ends((0, j), (1, j))
    middles((1, 1), (0, 1), (1, 2))

    own = jnp.concatenate([placing(flipped(me, j), own_target).astype(BF16) for j in range(groups)], axis=0)
    rows = jnp.concatenate([rows_ref[j, j * capacity : (j + 1) * capacity, :] for j in range(groups)], axis=0)
    resid_ref[...] = contract_rows(own, rows).astype(BF16)
    store(resid_ref, resid_hbm)
    for k in range(1, groups):
        gate_copies[k].wait_recv()
    gates = None
    for k in range(groups):
        one = plain(gate_in_ref[k, :, :capacity], placing(flipped(me, k), own_target).astype(BF16))
        gates = one if gates is None else gates + one
    dgates_ref[...] = gates[0:1, :].astype(BF16)

    row = lax.broadcasted_iota(jnp.int32, (chunk, chunk), 0)
    col = lax.broadcasted_iota(jnp.int32, (chunk, chunk), 1)

    def forward(h, carry):
        cols = pl.ds(pl.multiple_of(h * head_dim, head_dim), head_dim)
        state = prior_ref[h]
        for at in range(tokens // chunk):
            rows = pl.ds(at * chunk, chunk)
            keys, values, grads = key_ref[rows, cols], value_ref[rows, cols], grad_ref[rows, cols]
            mix = jnp.where(col <= row, contract_cols(grads, values), 0.0).astype(BF16)
            out = plain(mix, keys) + contract_cols(grads, state.astype(BF16))
            dquery_ref[rows, cols] = (out * inverse_counts(at * chunk, out.shape)).astype(BF16)
            state = state + contract_rows(keys, values)
        return carry

    def backward(h, carry):
        cols = pl.ds(pl.multiple_of(h * head_dim, head_dim), head_dim)
        state = line_ref[h]
        for at in reversed(range(tokens // chunk)):
            rows = pl.ds(at * chunk, chunk)
            query, keys = query_ref[rows, cols], key_ref[rows, cols]
            values, scaled = value_ref[rows, cols], scaled_grad_ref[rows, cols]
            held = state.astype(BF16)
            mix_key = jnp.where(col >= row, contract_cols(values, scaled), 0.0).astype(BF16)
            dkey_ref[rows, cols] = (plain(mix_key, query) + contract_cols(values, held)).astype(BF16)
            mix_value = jnp.where(col >= row, contract_cols(keys, query), 0.0).astype(BF16)
            dvalue_ref[rows, cols] = (plain(mix_value, scaled) + plain(keys, held)).astype(BF16)
            state = state + contract_rows(query, scaled)
        return carry

    loads[6].wait()
    for turn in range(len(steps)):
        take_state(turn)
        if turn + 1 < len(steps):
            send_state(turn + 1, 1 - last)
        if turn == 0:
            middles((0, 2))
            for j in range(3, length - 1):
                middles((1, j), (0, j))
            lax.fori_loop(0, heads, forward, 0)
            store(dquery_ref, dquery_hbm)
    if not steps:
        lax.fori_loop(0, heads, forward, 0)
        store(dquery_ref, dquery_hbm)
    across = len(steps)
    state_out_ref[across] = (line_ref[...] + local_ref[...] * side.astype(F32)).astype(BF16)
    state_copy(across, partner).start()
    state_copy(across, partner).wait_recv()
    line_ref[...] += state_in_ref[across].astype(F32)
    lax.fori_loop(0, heads, backward, 0)
    store(dkey_ref, dkey_hbm)
    store(dvalue_ref, dvalue_hbm)
    line_item(0, length - 1)
    store(up_ref, up_hbm)
    line_item(1, length - 1)
    store(down_ref, down_hbm)
    for copy in stores:
        copy.wait()
    for kind in range(2):
        for j in range(length - 1):
            line_copy(kind, j, 0, partner).wait_send()
    for turn in range(len(steps)):

        @pl.when(place >= steps[turn])
        def _():
            state_copy(turn, partner).wait_send()

    state_copy(across, partner).wait_send()
    sends.drain()


def pass_kernel(count, *refs):
    sources, targets, held, sems = refs[:count], refs[count : 2 * count], refs[2 * count : 3 * count], refs[3 * count]
    into, out_of = [], []
    for at in range(count):
        into.append(pltpu.make_async_copy(sources[at], held[at], sems.at[0, at]))
        into[-1].start()
    for at in range(count):
        into[at].wait()
        out_of.append(pltpu.make_async_copy(held[at], targets[at], sems.at[1, at]))
        out_of[-1].start()
    for copy in out_of:
        copy.wait()


def pass_on(*arrays):
    away = [pl.BlockSpec(memory_space=pl.ANY)] * len(arrays)
    return pl.pallas_call(
        functools.partial(pass_kernel, len(arrays)),
        in_specs=away,
        out_specs=away,
        out_shape=[jax.ShapeDtypeStruct(one.shape, one.dtype) for one in arrays],
        scratch_shapes=[pltpu.VMEM(one.shape, one.dtype) for one in arrays]
        + [pltpu.SemaphoreType.DMA((2, len(arrays)))],
        name="pass_on",
    )(*arrays)


def compute(
    attn_query, attn_key, attn_value, prefix_state, moe_in, grad_out, router_gates, expert_ids,
    w_gate_up, w_down, w_out,
):
    groups, blocks = lax.axis_size("exp"), lax.axis_size("ctx")
    rows, width = moe_in.shape
    capacity = 3 * rows // (2 * groups * w_gate_up.shape[0])
    hidden_units, wide = w_down.shape[1], w_gate_up.shape[2]
    unit, unit_down = width // blocks, hidden_units // blocks
    tokens, cols = attn_query.shape
    heads, head_dim = prefix_state.shape[1:3]
    length = blocks // 2
    turns = max(length.bit_length(), 1)
    direct = unit % LANES == 0
    whole = pl.BlockSpec(memory_space=pltpu.VMEM)
    away = pl.BlockSpec(memory_space=pl.ANY)
    flat = jax.ShapeDtypeStruct((tokens, cols), BF16)
    dma = pltpu.SemaphoreType.DMA
    vmem = pltpu.VMEM
    state = vmem((heads, head_dim, head_dim), F32)
    flat_ref = vmem((tokens, cols), BF16)
    scratch = [
        vmem((width, wide), BF16), vmem((hidden_units, width), BF16), vmem((cols, width), BF16),
        flat_ref, flat_ref, flat_ref, state, dma((7,)),
        flat_ref, flat_ref, flat_ref, vmem((rows, width), BF16), vmem((unit, wide), F32),
        vmem((unit_down, width), F32), dma((6,)),
        vmem((groups, 8, rows), jnp.int32), dma((2, groups)),
        vmem((groups - 1, capacity, 2 * width), BF16), vmem((groups, capacity, 2 * width), BF16),
        vmem((groups - 1, 16, LANES), BF16), vmem((groups, 16, LANES), BF16), dma((2, groups, 3)),
        vmem((2, 2 * capacity, width), BF16), vmem((2, 2 * capacity, wide), BF16),
        vmem((2, hidden_units, 2 * capacity), BF16),
        vmem((groups - 1, 16, LANES), BF16), vmem((groups, 16, LANES), BF16), dma((2, groups)),
        vmem((groups, groups * capacity, width), BF16), dma((2, groups, 3)),
        vmem((groups, groups * capacity, cols), BF16),
        flat_ref, flat_ref,
        state, state,
        vmem((turns, heads, head_dim, head_dim), BF16), vmem((turns, heads, head_dim, head_dim), BF16),
        dma((2, turns)),
        vmem((length, unit_down, width), BF16), vmem((length, unit_down, width), BF16), dma((2, 2, length)),
        vmem((length - 1, unit, wide), BF16), vmem((length + 1, unit, wide), BF16),
        vmem((length - 1, unit_down, width), BF16), vmem((length + 1, unit_down, width), BF16),
        dma((2, 2, length + 1)),
    ]
    if direct:
        scratch += [
            vmem((2, 2 * capacity, length * unit), BF16), vmem((2, 2 * capacity, wide), BF16),
            dma((2, groups * length + 3)),
        ]
    else:
        scratch += [
            vmem((2, width, 2 * capacity), BF16),
            vmem((length, unit, wide), BF16), vmem((length, unit, wide), BF16),
        ]
    found = pl.pallas_call(
        functools.partial(layer_kernel, groups, blocks, min(256, tokens), direct),
        in_specs=[whole] * 4 + [away] * 7,
        out_specs=[away] * 4 + [whole] + [away] * 2,
        out_shape=[
            flat, flat, flat, jax.ShapeDtypeStruct((rows, width), BF16), jax.ShapeDtypeStruct((1, rows), BF16),
            jax.ShapeDtypeStruct((unit, wide), F32), jax.ShapeDtypeStruct((unit_down, width), F32),
        ],
        scratch_shapes=scratch,
        compiler_params=pltpu.CompilerParams(
            collective_id=0, has_side_effects=True, vmem_limit_bytes=67043328
        ),
        name="layer",
    )(
        expert_ids.reshape(1, rows), router_gates.reshape(1, rows), moe_in, grad_out, w_gate_up[0], w_down[0], w_out,
        attn_query, attn_key, attn_value, prefix_state[0],
    )
    dquery, dkey, dvalue, resid, dgates, up, down = pass_on(*found)
    return dquery, dkey, dvalue, resid, dgates.reshape(rows, 1), up, down


def on_device(*args):
    dquery, dkey, dvalue, resid, dgates, up, down = compute(*args)
    return dquery, dkey, dvalue, resid, dgates, up[None], down[None]


def solution(mesh):
    return jax.shard_map(
        on_device,
        mesh=mesh,
        in_specs=(
            P("ctx", "exp"),
            P("ctx", "exp"),
            P("ctx", "exp"),
            P("ctx", "exp", None, None),
            P(("ctx", "exp"), None),
            P(("ctx", "exp"), None),
            P(("ctx", "exp"), None),
            P(("ctx", "exp"), None),
            P("exp", None, None),
            P("exp", None, None),
            P("exp", None),
        ),
        out_specs=(
            P("ctx", "exp"),
            P("ctx", "exp"),
            P("ctx", "exp"),
            P(("ctx", "exp"), None),
            P(("ctx", "exp"), None),
            P("exp", "ctx", None),
            P("exp", "ctx", None),
        ),
        check_vma=False,
    )
```

```python
import functools

import jax
import jax.numpy as jnp
from jax import lax
from jax.experimental import pallas as pl
from jax.experimental.pallas import tpu as pltpu
from jax.sharding import PartitionSpec as P

LANES = 128
MESH = pl.DeviceIdType.MESH
BF16 = jnp.bfloat16
F32 = jnp.float32


def contract_rows(left, right):
    return lax.dot_general(left, right, (((0,), (0,)), ((), ())), preferred_element_type=F32)


def contract_cols(left, right):
    return lax.dot_general(left, right, (((1,), (1,)), ((), ())), preferred_element_type=F32)


def plain(left, right):
    return jnp.dot(left, right, preferred_element_type=F32)


def bit_of(value, bit):
    return lax.rem(lax.div(value, bit), 2)


def flipped(value, mask):
    found, bit = value, 1
    while bit <= mask:
        if mask & bit:
            found = found + bit - 2 * bit * bit_of(value, bit)
        bit *= 2
    return found


def at_least(value, bound, size):
    return lax.div(value - bound + size, size)


class Sends:
    def __init__(self):
        self.open = []

    def start(self, src, dst, send, recv, device, when=None):
        copy = pltpu.make_async_remote_copy(
            src_ref=src, dst_ref=dst, send_sem=send, recv_sem=recv, device_id=device, device_id_type=MESH
        )
        self.open.append((copy, when))
        if when is None:
            copy.start()
        else:
            pl.when(when)(copy.start)
        return copy

    def drain(self):
        for copy, when in self.open:
            if when is None:
                copy.wait_send()
            else:
                pl.when(when)(copy.wait_send)


def layer_kernel(groups, blocks, chunk, direct, *refs):
    (
        ids_ref, gates_ref, moe_hbm, cot_hbm, pair_hbm, back_hbm, proj_hbm, query_hbm, key_hbm, value_hbm, prior_hbm,
        dquery_ref, dkey_ref, dvalue_ref, resid_ref, dgates_ref, up_ref, down_ref,
        moe_ref, cot_ref, pair_ref, back_ref, proj_ref, query_ref, key_ref, value_ref, prior_ref, load_sem,
        targets_ref, target_sem, packed_ref, came_ref, gate_packed_ref, gate_came_ref, token_sem,
        scaled_ref, both_ref, hidden_t_ref, gate_out_ref, gate_in_ref, gate_sem,
        rows_ref, rows_sem, slots_ref, grad_ref, scaled_grad_ref,
        local_ref, line_ref, state_out_ref, state_in_ref, state_sem,
        pair_down_out, pair_down_in, pair_sem,
        line_up_out, line_up_in, line_down_out, line_down_in, line_sem,
    ) = refs[:57+2]
    if direct:
        other_rows_ref, other_both_ref, other_sem = refs[57+2:]
    else:
        rows_t_ref, pair_up_out, pair_up_in = refs[57+2:]
    me, block = lax.axis_index("exp"), lax.axis_index("ctx")
    side, place = lax.rem(block, 2), lax.div(block, 2)
    length = blocks // 2
    tokens_own, width = moe_ref.shape
    capacity = came_ref.shape[1]
    hidden_units = back_ref.shape[0]
    heads, head_dim = prior_ref.shape[:2]
    tokens = query_ref.shape[0]
    unit, unit_down = width // blocks, hidden_units // blocks
    partner = {"ctx": block + 1 - 2 * side}
    sends = Sends()

    barrier = pltpu.get_barrier_semaphore()
    peers = [{"exp": flipped(me, k)} for k in range(1, groups)]
    shifts = [1]
    while shifts[-1] < blocks // 2:
        shifts.append(2 * shifts[-1])
    for shift in shifts:
        peers += [{"ctx": lax.rem(block + shift, blocks)}, {"ctx": lax.rem(block + blocks - shift, blocks)}]
    for peer in peers:
        pl.semaphore_signal(barrier, inc=1, device_id=peer, device_id_type=MESH)

    loads = []
    for at, (src, dst) in enumerate(
        [
            (moe_hbm, moe_ref), (cot_hbm, cot_ref), (pair_hbm, pair_ref), (back_hbm, back_ref), (proj_hbm, proj_ref), (query_hbm, query_ref),
            (key_hbm, key_ref), (value_hbm, value_ref), (prior_hbm, prior_ref),
        ]
    ):
        loads.append(pltpu.make_async_copy(src, dst, load_sem.at[at]))
        loads[-1].start()
    def near(k):
        return {"exp": flipped(me, k)}

    ids = ids_ref[...]
    experts = lax.broadcasted_iota(jnp.int32, (8, tokens_own), 0)
    member = jnp.where(experts == ids, 1.0, 0.0)
    earlier = jnp.where(
        lax.broadcasted_iota(jnp.int32, (tokens_own, tokens_own), 0)
        < lax.broadcasted_iota(jnp.int32, (tokens_own, tokens_own), 1), 1.0, 0.0,
    )
    slot = jnp.sum(plain(member.astype(BF16), earlier.astype(BF16)) * member, axis=0, keepdims=True)
    own_target = ids * capacity + slot.astype(jnp.int32)
    targets_ref[0] = jnp.broadcast_to(own_target, (8, tokens_own))
    gates_row = gates_ref[...].astype(F32)

    def placing(expert, targets):
        spots = lax.broadcasted_iota(jnp.int32, (capacity, tokens_own), 0) + expert * capacity
        return jnp.where(spots == targets, 1.0, 0.0)

    eye = jnp.where(
        lax.broadcasted_iota(jnp.int32, (capacity, LANES), 0) == lax.broadcasted_iota(jnp.int32, (capacity, LANES), 1),
        1.0, 0.0,
    )

    def as_row(column):
        return jnp.broadcast_to(jnp.sum(eye * column, axis=0, keepdims=True), (16, LANES)).astype(BF16)

    def as_column(rows):
        return jnp.sum(eye * rows[0:1, :].astype(F32), axis=1, keepdims=True)

    half = capacity // 2
    token_copies, target_copies, gate_copies_in = {}, {}, {}
    loads[0].wait()
    loads[1].wait()
    for k in (2, 3, 1, 0):
        found = placing(flipped(me, k), own_target)
        chosen = found.astype(BF16)
        out = packed_ref.at[k - 1] if k else came_ref.at[0]
        out[:, :width] = plain(chosen, moe_ref[...]).astype(BF16)
        out[:, width : 2 * width] = plain(chosen, cot_ref[...]).astype(BF16)
        gate_out = gate_packed_ref.at[k - 1] if k else gate_came_ref.at[0]
        gate_out[...] = as_row(jnp.sum(found * gates_row, axis=1, keepdims=True))
        if k == 2:
            pl.semaphore_wait(barrier, len(peers))
        if k:
            token_copies[k] = []
            cuts = [(0, capacity, 0)]
            cuts += [(0, half, width), (half, half, width)] if k == 3 else [(0, capacity, width)]
            for at, (begin, size, first) in enumerate(cuts):
                spots, cols = pl.ds(begin, size), pl.ds(first, width)
                if at == 1:
                    gate_copies_in[k] = sends.start(
                        gate_out, gate_came_ref.at[k], token_sem.at[0, k, 3], token_sem.at[1, k, 3], near(k)
                    )
                token_copies[k].append(
                    sends.start(
                        out.at[spots, cols], came_ref.at[k, spots, cols], token_sem.at[0, k, at],
                        token_sem.at[1, k, at], near(k),
                    )
                )
    for k in range(1, groups):
        target_copies[k] = sends.start(
            targets_ref.at[0], targets_ref.at[k], target_sem.at[0, k], target_sem.at[1, k], near(k)
        )

    gate_copies, row_copies, relay_copies, kept = {}, {}, {}, []
    other_copies = []

    def other(src, dst):
        at = len(other_copies)
        other_copies.append(sends.start(src, dst, other_sem.at[0, at], other_sem.at[1, at], partner))

    def expert(which, part, begin, piece, rows=(0, capacity), turn=0):
        spots_in = pl.ds(*rows)
        size = len(which) * rows[1]
        inner = pl.ds(begin + rows[0], size)
        for spot, k in enumerate(which):
            if k and not turn:
                token_copies[k][0].wait_recv()
            if direct and not turn:
                for home in range(length):
                    cols = pl.ds(pl.multiple_of((2 * home + 1 - side) * unit, unit), unit)
                    spots = pl.ds(begin + spot * capacity, capacity)
                    other(came_ref.at[k, :, cols], other_rows_ref.at[part, spots, pl.ds(home * unit, unit)])
        rows_in = jnp.concatenate([came_ref[k, spots_in, :width] for k in which], axis=0)
        both = plain(rows_in, pair_ref[...])
        first, second = both[:, :hidden_units], both[:, hidden_units:]
        logistic = jax.nn.sigmoid(first)
        silu = first * logistic
        hidden = (silu * second).astype(BF16)
        slope = logistic * (1.0 + first * (1.0 - logistic))
        for k in which:
            if k:
                if not turn:
                    gate_copies_in[k].wait_recv()
                token_copies[k][1 + turn].wait_recv()
        cot = jnp.concatenate([came_ref[k, spots_in, width : 2 * width] for k in which], axis=0).astype(F32)
        gate = jnp.concatenate([as_column(gate_came_ref[k])[rows[0] : rows[0] + rows[1]] for k in which], axis=0)
        scaled = (gate * cot).astype(BF16)
        scaled_ref[part, inner, :] = scaled
        grad_hidden = contract_cols(scaled, back_ref[...])
        both_ref[part, inner, :hidden_units] = (grad_hidden * second * slope).astype(BF16)
        both_ref[part, inner, hidden_units:] = (grad_hidden * silu).astype(BF16)
        if direct:
            other(both_ref.at[part, inner], other_both_ref.at[part, inner])
        grad_rows = contract_cols(both_ref[part, inner, :], pair_ref[...]).astype(BF16)
        at = pl.ds(part * 2 * capacity + begin + rows[0], size)
        rows_ref[0, at, :] = (cot + grad_rows.astype(F32)).astype(BF16)
        at = pl.ds(part * 2 * capacity + begin, len(which) * capacity)
        done = rows[0] + rows[1] == capacity
        for peer in (2, 1) if done else ():
            row_copies[peer, piece] = sends.start(
                rows_ref.at[0, at], rows_ref.at[peer, at],
                rows_sem.at[0, peer, piece], rows_sem.at[1, peer, piece], near(peer),
            )
        output = plain(hidden, back_ref[...])
        grad_gate = jnp.sum(cot * output, axis=1, keepdims=True)
        if kept:
            grad_gate = jnp.concatenate([kept.pop(), grad_gate], axis=0)
        if not done:
            kept.append(grad_gate)
        for spot, k in enumerate(which) if done else ():
            one = as_row(grad_gate[spot * capacity : (spot + 1) * capacity])
            if k:
                gate_out_ref[k - 1] = one
                gate_copies[k] = sends.start(
                    gate_out_ref.at[k - 1], gate_in_ref.at[k], gate_sem.at[0, k], gate_sem.at[1, k], near(k)
                )
            else:
                gate_in_ref[0] = one
        return hidden

    pieces = [pl.ds(0, 2 * capacity), pl.ds(2 * capacity, capacity), pl.ds(3 * capacity, capacity)]

    def project(j, piece):
        slots_ref[j, pieces[piece], :] = contract_cols(rows_ref[j, pieces[piece], :], proj_ref[...]).astype(BF16)

    def project_near(piece):
        project(0, piece)
        row_copies[1, piece].wait_recv()
        project(1, piece)

    def project_far(piece):
        row_copies[2, piece].wait_recv()
        relay_copies[piece] = sends.start(
            rows_ref.at[2, pieces[piece]], rows_ref.at[3, pieces[piece]],
            rows_sem.at[0, 3, piece], rows_sem.at[1, 3, piece], near(1),
        )
        project(2, piece)
        relay_copies[piece].wait_recv()
        project(3, piece)

    loads[2].wait()
    loads[3].wait()
    hidden_t_ref[0] = expert((0, 1), 0, 0, 0).T
    if not direct:
        rows_t_ref[0] = jnp.concatenate([came_ref[0, :, :width], came_ref[1, :, :width]], axis=0).T
    loads[4].wait()
    project_near(0)
    hidden_2 = expert((2,), 1, 0, 1)
    project_near(1)
    hidden_3 = expert((3,), 1, capacity, 2, (0, half))
    hidden_4 = expert((3,), 1, capacity, 2, (half, half), 1)
    hidden_t_ref[1] = jnp.concatenate([hidden_2, hidden_3, hidden_4], axis=0).T
    if not direct:
        rows_t_ref[1] = jnp.concatenate([came_ref[2, :, :width], came_ref[3, :, :width]], axis=0).T

    wide = both_ref.shape[2]
    columns = {0: pl.ds(0, wide // 2), 2: pl.ds(wide // 2, wide // 2)}

    def up_rows(which, over):
        at = pl.ds(pl.multiple_of(which * unit, unit), unit)
        return plain(rows_t_ref[0, at, :], both_ref[0, :, over]) + plain(rows_t_ref[1, at, :], both_ref[1, :, over])

    def up_pair(kind, j, home):
        over = columns[kind]
        if not direct:
            if kind == 0:
                pair_copies[0, j].wait_recv()
            return up_rows(2 * home + side, over) + pair_up_in[j, :, over].astype(F32)
        cols = pl.ds(pl.multiple_of((2 * home + side) * unit, unit), unit)
        there = pl.ds(pl.multiple_of(home * unit, unit), unit)
        found = None
        for part in range(2):
            here = jnp.concatenate([came_ref[2 * part, :, cols], came_ref[2 * part + 1, :, cols]], axis=0)
            one = contract_rows(here, both_ref[part, :, over])
            one = one + contract_rows(other_rows_ref[part, :, there], other_both_ref[part, :, over])
            found = one if found is None else found + one
        return found

    def down_rows(which):
        at = pl.ds(pl.multiple_of(which * unit_down, unit_down), unit_down)
        return plain(hidden_t_ref[0, at, :], scaled_ref[0]) + plain(hidden_t_ref[1, at, :], scaled_ref[1])

    right_half = lax.div(place, max(length // 2, 1))
    fewer = place * (1 - right_half) + (length - 1 - place) * right_half

    def item(j):
        both_ways = at_least(2 * fewer, j + 1, 4 * length)
        step = both_ways * (j // 2) + (1 - both_ways) * (j - fewer)
        major = 1 - both_ways * (j % 2)
        rightward = major * (1 - right_half) + (1 - major) * right_half
        return rightward * (length - 1 - step) + (1 - rightward) * step, rightward

    items = [item(j) for j in range(length - 1)] + [(place, None)]
    pair_copies = {}

    def pair_sends():
        for j, (home, _) in enumerate(items):
            if not direct:
                pair_up_out[j] = up_rows(2 * home + 1 - side, pl.ds(0, wide)).astype(BF16)
                pair_copies[0, j] = sends.start(
                    pair_up_out.at[j], pair_up_in.at[j], pair_sem.at[0, 0, j], pair_sem.at[1, 0, j], partner
                )
            pair_down_out[j] = down_rows(2 * home + 1 - side).astype(BF16)
            pair_copies[1, j] = sends.start(
                pair_down_out.at[j], pair_down_in.at[j], pair_sem.at[0, 1, j], pair_sem.at[1, 1, j], partner
            )

    has_left, has_right = at_least(place, 1, 2 * length), at_least(length - 1 - place, 1, 2 * length)
    inside = has_left * has_right

    def line_copy(kind, j, slot, device):
        if kind == 1:
            src, dst = line_down_out.at[j], line_down_in.at[slot]
        else:
            src, dst = line_up_out.at[j, :, columns[kind]], line_up_in.at[slot, :, columns[kind]]
        return pltpu.make_async_remote_copy(
            src_ref=src, dst_ref=dst, send_sem=line_sem.at[0, kind, j], recv_sem=line_sem.at[1, kind, slot],
            device_id=device, device_id_type=MESH,
        )

    def line_item(kind, j):
        home, rightward = items[j]
        if kind == 1:
            over, total, out, line_in = slice(None), down_ref, line_down_out, line_down_in
            pair_copies[1, j].wait_recv()
            total[...] = down_rows(2 * home + side) + pair_down_in[j].astype(F32)
        else:
            over, total, out, line_in = columns[kind], up_ref, line_up_out, line_up_in
            total[:, over] = up_pair(kind, j, home)
        if rightward is None:
            ways = [(has_left, place + 1), (has_right, place)]
        else:
            ways = [(rightward * has_left + (1 - rightward) * has_right, home + rightward)]
        for present, slot in ways:

            @pl.when(present == 1)
            def _():
                line_copy(kind, 0, slot, partner).wait_recv()
                total[:, over] += line_in[slot, :, over].astype(F32)

        if rightward is not None:
            out[j, :, over] = total[:, over].astype(BF16)
            line_copy(kind, j, home + rightward, {"ctx": block + 4 * rightward - 2}).start()

    def ends(*which, last=False):
        @pl.when(inside == 0)
        def _():
            for kind, j in which:
                if last or j < length - 1:
                    line_item(kind, j)

    def middles(*which, last=False):
        @pl.when(inside == 1)
        def _():
            for kind, j in which:
                if last or j < length - 1:
                    line_item(kind, j)

    pair_sends()
    for copy in other_copies:
        copy.wait_recv()
    ends((0, 0), (2, 0))
    project_near(2)
    ends((1, 0), (0, 1), (2, 1))
    middles((0, 0), (2, 0))
    project_far(0)
    ends((1, 1))
    middles((1, 0), (0, 1), (2, 1))
    project_far(1)
    middles((0, 2), (1, 1))
    project_far(2)
    middles((2, 2))

    base = (3 * blocks + block) * tokens
    for at in (5, 6, 7):
        loads[at].wait()

    def inverse_counts(start, shape):
        counts = base + start + 1 + lax.broadcasted_iota(jnp.int32, shape, 0)
        return 1.0 / counts.astype(F32)

    for i in range(groups):
        if i:
            target_copies[i].wait_recv()
        targets = targets_ref[i, 0:1, :]
        chosen = jnp.concatenate([placing(flipped(me, j), targets).astype(BF16) for j in range(groups)], axis=0)
        found = jnp.concatenate(
            [slots_ref[j, (j ^ i) * capacity : ((j ^ i) + 1) * capacity, :] for j in range(groups)], axis=0
        )
        start = pl.multiple_of(flipped(me, i) * tokens_own, tokens_own)
        at = pl.ds(start, tokens_own)
        grads = contract_rows(chosen, found)
        scaled = (grads * inverse_counts(start, grads.shape)).astype(BF16)
        grad_ref[at, :] = grads.astype(BF16)
        scaled_grad_ref[at, :] = scaled
        for h in range(heads):
            cols = slice(h * head_dim, (h + 1) * head_dim)
            state = contract_rows(query_ref[at, cols], scaled[:, cols])
            local_ref[h] = state + local_ref[h] if i else state

    cuts = [(0, heads // 2), (heads // 2, heads - heads // 2)] if heads > 1 else [(0, heads)]

    def state_copy(turn, at, device):
        part = pl.ds(*cuts[at])
        return pltpu.make_async_remote_copy(
            src_ref=state_out_ref.at[turn, part], dst_ref=state_in_ref.at[turn, part],
            send_sem=state_sem.at[0, turn, at], recv_sem=state_sem.at[1, turn, at],
            device_id=device, device_id_type=MESH,
        )

    line_ref[...] = jnp.zeros_like(line_ref)

    def send_state(chosen, at):
        @pl.when(chosen * has_left == 1)
        def _():
            part = pl.ds(*cuts[at])
            state_out_ref[0, part] = (local_ref[part] + line_ref[part]).astype(BF16)
            state_copy(0, at, {"ctx": lax.rem(block + blocks - 2, blocks)}).start()

    for at in range(len(cuts)):
        send_state(1 - has_right, at)
    for j in range(2, length - 1):
        ends((0, j), (2, j), (1, j))

    own = jnp.concatenate([placing(flipped(me, j), own_target).astype(BF16) for j in range(groups)], axis=0)
    rows = jnp.concatenate([rows_ref[j, j * capacity : (j + 1) * capacity, :] for j in range(groups)], axis=0)
    resid_ref[...] = contract_rows(own, rows).astype(BF16)
    for k in range(1, groups):
        gate_copies[k].wait_recv()
    gates = None
    for k in range(groups):
        one = plain(gate_in_ref[k, :, :capacity], placing(flipped(me, k), own_target).astype(BF16))
        gates = one if gates is None else gates + one
    dgates_ref[...] = gates[0:1, :].astype(BF16)

    row = lax.broadcasted_iota(jnp.int32, (chunk, chunk), 0)
    col = lax.broadcasted_iota(jnp.int32, (chunk, chunk), 1)

    def forward(h, carry):
        cols = pl.ds(pl.multiple_of(h * head_dim, head_dim), head_dim)
        state = prior_ref[h]
        for at in range(tokens // chunk):
            rows = pl.ds(at * chunk, chunk)
            keys, values, grads = key_ref[rows, cols], value_ref[rows, cols], grad_ref[rows, cols]
            mix = jnp.where(col <= row, contract_cols(grads, values), 0.0).astype(BF16)
            out = plain(mix, keys) + contract_cols(grads, state.astype(BF16))
            dquery_ref[rows, cols] = (out * inverse_counts(at * chunk, out.shape)).astype(BF16)
            state = state + contract_rows(keys, values)
        return carry

    def backward(h, carry):
        cols = pl.ds(pl.multiple_of(h * head_dim, head_dim), head_dim)
        state = line_ref[h]
        for at in reversed(range(tokens // chunk)):
            rows = pl.ds(at * chunk, chunk)
            query, keys = query_ref[rows, cols], key_ref[rows, cols]
            values, scaled = value_ref[rows, cols], scaled_grad_ref[rows, cols]
            held = state.astype(BF16)
            mix_key = jnp.where(col >= row, contract_cols(values, scaled), 0.0).astype(BF16)
            dkey_ref[rows, cols] = (plain(mix_key, query) + contract_cols(values, held)).astype(BF16)
            mix_value = jnp.where(col >= row, contract_cols(keys, query), 0.0).astype(BF16)
            dvalue_ref[rows, cols] = (plain(mix_value, scaled) + plain(keys, held)).astype(BF16)
            state = state + contract_rows(query, scaled)
        return carry

    loads[8].wait()
    lax.fori_loop(0, heads, forward, 0)
    for at, cut in enumerate(cuts):
        part = pl.ds(*cut)

        @pl.when(has_right == 1)
        def _():
            state_copy(0, at, partner).wait_recv()
            line_ref[part] = state_in_ref[0, part].astype(F32)

        send_state(has_right, at)
        state_out_ref[1, part] = (line_ref[part] + local_ref[part] * side.astype(F32)).astype(BF16)
        state_copy(1, at, partner).start()
    middles((1, 2))
    for j in range(3, length - 1):
        middles((0, j), (2, j), (1, j))
    finals = [(0, length - 1), (2, length - 1), (1, length - 1)]
    ends(*finals, last=True)
    for at, (begin, size) in enumerate(cuts):
        part = pl.ds(begin, size)
        state_copy(1, at, partner).wait_recv()
        line_ref[part] += state_in_ref[1, part].astype(F32)
        lax.fori_loop(begin, begin + size, backward, 0)
    middles(*finals, last=True)
    for kind in range(3):
        for j in range(length - 1):
            line_copy(kind, j, 0, partner).wait_send()

    for at in range(len(cuts)):

        @pl.when(has_left == 1)
        def _():
            state_copy(0, at, partner).wait_send()

        state_copy(1, at, partner).wait_send()
    sends.drain()


def pass_kernel(count, *refs):
    sems = refs[2 * count]
    copies = [pltpu.make_async_copy(refs[at], refs[count + at], sems.at[at]) for at in range(count)]
    for copy in copies:
        copy.start()
    for copy in copies:
        copy.wait()


def pass_on(*arrays):
    return pl.pallas_call(
        functools.partial(pass_kernel, len(arrays)),
        in_specs=[pl.BlockSpec(memory_space=pltpu.VMEM)] * len(arrays),
        out_specs=[pl.BlockSpec(memory_space=pl.ANY)] * len(arrays),
        out_shape=[jax.ShapeDtypeStruct(one.shape, one.dtype) for one in arrays],
        scratch_shapes=[pltpu.SemaphoreType.DMA((len(arrays),))],
        compiler_params=pltpu.CompilerParams(vmem_limit_bytes=1 << 20),
        name="pass_on",
    )(*[pltpu.with_memory_space_constraint(one, pltpu.VMEM) for one in arrays])


def compute(
    attn_query, attn_key, attn_value, prefix_state, moe_in, grad_out, router_gates, expert_ids,
    w_gate_up, w_down, w_out,
):
    groups, blocks = lax.axis_size("exp"), lax.axis_size("ctx")
    rows, width = moe_in.shape
    capacity = 3 * rows // (2 * groups * w_gate_up.shape[0])
    hidden_units, wide = w_down.shape[1], w_gate_up.shape[2]
    unit, unit_down = width // blocks, hidden_units // blocks
    tokens, cols = attn_query.shape
    heads, head_dim = prefix_state.shape[1:3]
    length = blocks // 2
    turns = 2
    direct = unit % LANES == 0
    whole = pl.BlockSpec(memory_space=pltpu.VMEM)
    away = pl.BlockSpec(memory_space=pl.ANY)
    dma = pltpu.SemaphoreType.DMA
    vmem = pltpu.VMEM
    state = vmem((heads, head_dim, head_dim), F32)
    flat_ref = vmem((tokens, cols), BF16)
    scratch = [
        vmem((rows, width), BF16), vmem((rows, width), BF16),
        vmem((width, wide), BF16), vmem((hidden_units, width), BF16), vmem((cols, width), BF16),
        flat_ref, flat_ref, flat_ref, state, dma((9,)),
        vmem((groups, 8, rows), jnp.int32), dma((2, groups)),
        vmem((groups - 1, capacity, 2 * width), BF16), vmem((groups, capacity, 2 * width), BF16),
        vmem((groups - 1, 16, LANES), BF16), vmem((groups, 16, LANES), BF16), dma((2, groups, 4)),
        vmem((2, 2 * capacity, width), BF16), vmem((2, 2 * capacity, wide), BF16),
        vmem((2, hidden_units, 2 * capacity), BF16),
        vmem((groups - 1, 16, LANES), BF16), vmem((groups, 16, LANES), BF16), dma((2, groups)),
        vmem((groups, groups * capacity, width), BF16), dma((2, groups, 3)),
        vmem((groups, groups * capacity, cols), BF16),
        flat_ref, flat_ref,
        state, state,
        vmem((turns, heads, head_dim, head_dim), BF16), vmem((turns, heads, head_dim, head_dim), BF16),
        dma((2, turns, 2)),
        vmem((length, unit_down, width), BF16), vmem((length, unit_down, width), BF16), dma((2, 2, length)),
        vmem((length - 1, unit, wide), BF16), vmem((length + 1, unit, wide), BF16),
        vmem((length - 1, unit_down, width), BF16), vmem((length + 1, unit_down, width), BF16),
        dma((2, 3, length + 1)),
    ]
    if direct:
        scratch += [
            vmem((2, 2 * capacity, length * unit), BF16), vmem((2, 2 * capacity, wide), BF16),
            dma((2, groups * length + 4)),
        ]
    else:
        scratch += [
            vmem((2, width, 2 * capacity), BF16),
            vmem((length, unit, wide), BF16), vmem((length, unit, wide), BF16),
        ]
    found = pl.pallas_call(
        functools.partial(layer_kernel, groups, blocks, min(256, tokens), direct),
        in_specs=[whole] * 2 + [away] * 9,
        out_specs=[whole] * 7,
        out_shape=[
            flat_ref, flat_ref, flat_ref, vmem((rows, width), BF16), vmem((1, rows), BF16),
            vmem((unit, wide), F32), vmem((unit_down, width), F32),
        ],
        scratch_shapes=scratch,
        compiler_params=pltpu.CompilerParams(
            collective_id=0, has_side_effects=True, vmem_limit_bytes=56000000
        ),
        name="layer",
    )(
        expert_ids.reshape(1, rows), router_gates.reshape(1, rows), moe_in, grad_out, w_gate_up[0], w_down[0], w_out,
        attn_query, attn_key, attn_value, prefix_state[0],
    )
    dquery, dkey, dvalue, resid, dgates, up, down = pass_on(*found)
    return dquery, dkey, dvalue, resid, dgates.reshape(rows, 1), up, down


def on_device(*args):
    dquery, dkey, dvalue, resid, dgates, up, down = compute(*args)
    return dquery, dkey, dvalue, resid, dgates, up[None], down[None]


def solution(mesh):
    return jax.shard_map(
        on_device,
        mesh=mesh,
        in_specs=(
            P("ctx", "exp"),
            P("ctx", "exp"),
            P("ctx", "exp"),
            P("ctx", "exp", None, None),
            P(("ctx", "exp"), None),
            P(("ctx", "exp"), None),
            P(("ctx", "exp"), None),
            P(("ctx", "exp"), None),
            P("exp", None, None),
            P("exp", None, None),
            P("exp", None),
        ),
        out_specs=(
            P("ctx", "exp"),
            P("ctx", "exp"),
            P("ctx", "exp"),
            P(("ctx", "exp"), None),
            P(("ctx", "exp"), None),
            P("exp", "ctx", None),
            P("exp", "ctx", None),
        ),
        check_vma=False,
    )
```

```python
import functools

import jax
import jax.numpy as jnp
from jax import lax
from jax.experimental import pallas as pl
from jax.experimental.pallas import tpu as pltpu
from jax.sharding import PartitionSpec as P

LANES = 128
MESH = pl.DeviceIdType.MESH
BF16 = jnp.bfloat16
F32 = jnp.float32


def contract_rows(left, right):
    return lax.dot_general(left, right, (((0,), (0,)), ((), ())), preferred_element_type=F32)


def contract_cols(left, right):
    return lax.dot_general(left, right, (((1,), (1,)), ((), ())), preferred_element_type=F32)


def plain(left, right):
    return jnp.dot(left, right, preferred_element_type=F32)


def bit_of(value, bit):
    return lax.rem(lax.div(value, bit), 2)


def flipped(value, mask):
    found, bit = value, 1
    while bit <= mask:
        if mask & bit:
            found = found + bit - 2 * bit * bit_of(value, bit)
        bit *= 2
    return found


def at_least(value, bound, size):
    return lax.div(value - bound + size, size)


class Sends:
    def __init__(self):
        self.open = []

    def start(self, src, dst, send, recv, device, when=None):
        copy = pltpu.make_async_remote_copy(
            src_ref=src, dst_ref=dst, send_sem=send, recv_sem=recv, device_id=device, device_id_type=MESH
        )
        self.open.append((copy, when))
        if when is None:
            copy.start()
        else:
            pl.when(when)(copy.start)
        return copy

    def drain(self):
        pending, self.open = self.open, []
        for copy, when in pending:
            if when is None:
                copy.wait_send()
            else:
                pl.when(when)(copy.wait_send)


def layer_kernel(groups, blocks, chunk, direct, *refs):
    (
        ids_ref, gates_ref, moe_hbm, cot_hbm, pair_hbm, back_hbm, proj_hbm, query_hbm, key_hbm, value_hbm, prior_hbm,
        dquery_ref, dkey_ref, dvalue_ref, resid_ref, dgates_ref, up_ref, down_ref,
        moe_ref, cot_ref, pair_ref, back_ref, proj_ref, query_ref, key_ref, value_ref, prior_ref, load_sem,
        targets_ref, target_sem, packed_ref, came_ref, gate_packed_ref, gate_came_ref, token_sem,
        scaled_ref, both_ref, hidden_t_ref, gate_out_ref, gate_in_ref, gate_sem,
        rows_ref, rows_sem, slots_ref, grad_ref, scaled_grad_ref,
        local_ref, line_ref, later_ref, state_out_ref, state_in_ref, state_sem,
        pair_down_out, pair_down_in, pair_sem,
        line_up_out, line_up_in, line_down_out, line_down_in, line_sem,
    ) = refs[:60]
    if direct:
        other_rows_ref, other_both_ref, other_sem = refs[60:]
    else:
        rows_t_ref, pair_up_out, pair_up_in = refs[60:]
    me, block = lax.axis_index("exp"), lax.axis_index("ctx")
    side, place = lax.rem(block, 2), lax.div(block, 2)
    length = blocks // 2
    tokens_own, width = moe_ref.shape
    capacity = came_ref.shape[1]
    hidden_units = back_ref.shape[0]
    heads, head_dim = prior_ref.shape[:2]
    tokens = query_ref.shape[0]
    unit, unit_down = width // blocks, hidden_units // blocks
    partner = {"ctx": block + 1 - 2 * side}
    sends = Sends()

    loads = []
    for at, (src, dst) in enumerate(
        [
            (moe_hbm, moe_ref), (cot_hbm, cot_ref), (pair_hbm, pair_ref), (back_hbm, back_ref), (proj_hbm, proj_ref), (query_hbm, query_ref),
            (key_hbm, key_ref), (value_hbm, value_ref), (prior_hbm, prior_ref),
        ]
    ):
        loads.append(pltpu.make_async_copy(src, dst, load_sem.at[at]))
    loads[0].start()
    loads[1].start()
    barrier = pltpu.get_barrier_semaphore()
    peers = [{"exp": flipped(me, k)} for k in range(1, groups)]
    shifts = (1, 2, 3)
    for shift in shifts:
        peers += [{"ctx": lax.rem(block + shift, blocks)}, {"ctx": lax.rem(block + blocks - shift, blocks)}]
    for peer in peers:
        pl.semaphore_signal(barrier, inc=1, device_id=peer, device_id_type=MESH)

    def near(k):
        return {"exp": flipped(me, k)}

    ids = ids_ref[...]
    experts = lax.broadcasted_iota(jnp.int32, (8, tokens_own), 0)
    member = jnp.where(experts == ids, 1.0, 0.0)
    earlier = jnp.where(
        lax.broadcasted_iota(jnp.int32, (tokens_own, tokens_own), 0)
        < lax.broadcasted_iota(jnp.int32, (tokens_own, tokens_own), 1), 1.0, 0.0,
    )
    slot = jnp.sum(plain(member.astype(BF16), earlier.astype(BF16)) * member, axis=0, keepdims=True)
    own_target = ids * capacity + slot.astype(jnp.int32)
    targets_ref[0] = jnp.broadcast_to(own_target, (8, tokens_own))
    gates_row = gates_ref[...].astype(F32)

    def placing(expert, targets):
        spots = lax.broadcasted_iota(jnp.int32, (capacity, tokens_own), 0) + expert * capacity
        return jnp.where(spots == targets, 1.0, 0.0)

    eye = jnp.where(
        lax.broadcasted_iota(jnp.int32, (capacity, LANES), 0) == lax.broadcasted_iota(jnp.int32, (capacity, LANES), 1),
        1.0, 0.0,
    )

    def as_row(column):
        return jnp.broadcast_to(jnp.sum(eye * column, axis=0, keepdims=True), (16, LANES)).astype(BF16)

    def as_column(rows):
        return jnp.sum(eye * rows[0:1, :].astype(F32), axis=1, keepdims=True)

    half = 2 * capacity // 3 // 16 * 16
    token_copies, target_copies, gate_copies_in = {}, {}, {}
    loads[0].wait()
    for k in (2, 3, 1, 0):
        found = placing(flipped(me, k), own_target)
        chosen = found.astype(BF16)
        out = packed_ref.at[k - 1] if k else came_ref.at[0]
        gate_out = gate_packed_ref.at[k - 1] if k else gate_came_ref.at[0]
        token_copies[k] = []

        def send_tokens(begin, size, first):
            spots, cols, at = pl.ds(begin, size), pl.ds(first, width), len(token_copies[k])
            token_copies[k].append(
                sends.start(
                    out.at[spots, cols], came_ref.at[k, spots, cols], token_sem.at[0, k, at],
                    token_sem.at[1, k, at], near(k),
                )
            )

        out[:, :width] = plain(chosen, moe_ref[...]).astype(BF16)
        if k == 2:
            pl.semaphore_wait(barrier, len(peers))
        if k:
            send_tokens(0, capacity, 0)
        gate_out[...] = as_row(jnp.sum(found * gates_row, axis=1, keepdims=True))
        if k == 2:
            loads[1].wait()
            for load in loads[2:]:
                load.start()
        out[:, width : 2 * width] = plain(chosen, cot_ref[...]).astype(BF16)
        if k:
            gate_copies_in[k] = sends.start(
                gate_out, gate_came_ref.at[k], token_sem.at[0, k, 3], token_sem.at[1, k, 3], near(k)
            )
            for begin, size in ((0, half), (half, capacity - half)) if k == 3 else ((0, capacity),):
                send_tokens(begin, size, width)
    for k in range(1, groups):
        target_copies[k] = sends.start(
            targets_ref.at[0], targets_ref.at[k], target_sem.at[0, k], target_sem.at[1, k], near(k)
        )

    gate_copies, row_copies, relay_copies, kept = {}, {}, {}, []
    other_copies = []

    def other(src, dst):
        at = len(other_copies)
        other_copies.append(sends.start(src, dst, other_sem.at[0, at], other_sem.at[1, at], partner))

    def expert(which, part, begin, piece, rows=(0, capacity), turn=0):
        spots_in = pl.ds(*rows)
        size = len(which) * rows[1]
        inner = pl.ds(begin + rows[0], size)
        for spot, k in enumerate(which):
            if k and not turn:
                token_copies[k][0].wait_recv()
            if direct and not turn:
                for home in range(length):
                    cols = pl.ds(pl.multiple_of((2 * home + 1 - side) * unit, unit), unit)
                    spots = pl.ds(begin + spot * capacity, capacity)
                    other(came_ref.at[k, :, cols], other_rows_ref.at[part, spots, pl.ds(home * unit, unit)])
        rows_in = jnp.concatenate([came_ref[k, spots_in, :width] for k in which], axis=0)
        both = plain(rows_in, pair_ref[...])
        first, second = both[:, :hidden_units], both[:, hidden_units:]
        logistic = jax.nn.sigmoid(first)
        silu = first * logistic
        hidden = (silu * second).astype(BF16)
        slope = logistic * (1.0 + first * (1.0 - logistic))
        for k in which:
            if k:
                if not turn:
                    gate_copies_in[k].wait_recv()
                token_copies[k][1 + turn].wait_recv()
        cot = jnp.concatenate([came_ref[k, spots_in, width : 2 * width] for k in which], axis=0).astype(F32)
        gate = jnp.concatenate([as_column(gate_came_ref[k])[rows[0] : rows[0] + rows[1]] for k in which], axis=0)
        scaled = (gate * cot).astype(BF16)
        scaled_ref[part, inner, :] = scaled
        grad_hidden = contract_cols(scaled, back_ref[...])
        both_ref[part, inner, :hidden_units] = (grad_hidden * second * slope).astype(BF16)
        both_ref[part, inner, hidden_units:] = (grad_hidden * silu).astype(BF16)
        if direct:
            other(both_ref.at[part, inner], other_both_ref.at[part, inner])
        grad_rows = contract_cols(both_ref[part, inner, :], pair_ref[...]).astype(BF16)
        at = pl.ds(part * 2 * capacity + begin + rows[0], size)
        rows_ref[0, at, :] = (cot + grad_rows.astype(F32)).astype(BF16)
        at = pl.ds(part * 2 * capacity + begin, len(which) * capacity)
        done = rows[0] + rows[1] == capacity
        for peer in (2, 1) if done else ():
            row_copies[peer, piece] = sends.start(
                rows_ref.at[0, at], rows_ref.at[peer, at],
                rows_sem.at[0, peer, piece], rows_sem.at[1, peer, piece], near(peer),
            )
        output = plain(hidden, back_ref[...])
        grad_gate = jnp.sum(cot * output, axis=1, keepdims=True)
        if kept:
            grad_gate = jnp.concatenate([kept.pop(), grad_gate], axis=0)
        if not done:
            kept.append(grad_gate)
        for spot, k in enumerate(which) if done else ():
            one = as_row(grad_gate[spot * capacity : (spot + 1) * capacity])
            if k:
                gate_out_ref[k - 1] = one
                gate_copies[k] = sends.start(
                    gate_out_ref.at[k - 1], gate_in_ref.at[k], gate_sem.at[0, k], gate_sem.at[1, k], near(k)
                )
            else:
                gate_in_ref[0] = one
        return hidden

    pieces = [pl.ds(0, 2 * capacity), pl.ds(2 * capacity, capacity), pl.ds(3 * capacity, capacity)]

    def project(j, piece):
        slots_ref[j, pieces[piece], :] = contract_cols(rows_ref[j, pieces[piece], :], proj_ref[...]).astype(BF16)

    def project_near(piece):
        project(0, piece)
        row_copies[1, piece].wait_recv()
        project(1, piece)

    def project_far(piece):
        row_copies[2, piece].wait_recv()
        relay_copies[piece] = sends.start(
            rows_ref.at[2, pieces[piece]], rows_ref.at[3, pieces[piece]],
            rows_sem.at[0, 3, piece], rows_sem.at[1, 3, piece], near(1),
        )
        project(2, piece)
        relay_copies[piece].wait_recv()
        project(3, piece)

    loads[2].wait()
    loads[3].wait()
    hidden_t_ref[0] = expert((0, 1), 0, 0, 0).T
    if not direct:
        rows_t_ref[0] = jnp.concatenate([came_ref[0, :, :width], came_ref[1, :, :width]], axis=0).T
    loads[4].wait()
    project_near(0)
    hidden_2 = expert((2,), 1, 0, 1)
    project_near(1)
    hidden_3 = expert((3,), 1, capacity, 2, (0, half))
    hidden_4 = expert((3,), 1, capacity, 2, (half, capacity - half), 1)
    hidden_t_ref[1] = jnp.concatenate([hidden_2, hidden_3, hidden_4], axis=0).T
    if not direct:
        rows_t_ref[1] = jnp.concatenate([came_ref[2, :, :width], came_ref[3, :, :width]], axis=0).T

    wide = both_ref.shape[2]
    columns = {0: pl.ds(0, wide // 2), 2: pl.ds(wide // 2, wide // 2)}

    def up_rows(which, over):
        at = pl.ds(pl.multiple_of(which * unit, unit), unit)
        return plain(rows_t_ref[0, at, :], both_ref[0, :, over]) + plain(rows_t_ref[1, at, :], both_ref[1, :, over])

    def up_pair(kind, j, home):
        over = columns[kind]
        if not direct:
            if kind == 0:
                pair_copies[0, j].wait_recv()
            return up_rows(2 * home + side, over) + pair_up_in[j, :, over].astype(F32)
        cols = pl.ds(pl.multiple_of((2 * home + side) * unit, unit), unit)
        there = pl.ds(pl.multiple_of(home * unit, unit), unit)
        found = None
        for part in range(2):
            here = jnp.concatenate([came_ref[2 * part, :, cols], came_ref[2 * part + 1, :, cols]], axis=0)
            one = contract_rows(here, both_ref[part, :, over])
            one = one + contract_rows(other_rows_ref[part, :, there], other_both_ref[part, :, over])
            found = one if found is None else found + one
        return found

    def down_rows(which):
        at = pl.ds(pl.multiple_of(which * unit_down, unit_down), unit_down)
        return plain(hidden_t_ref[0, at, :], scaled_ref[0]) + plain(hidden_t_ref[1, at, :], scaled_ref[1])

    right_half = lax.div(place, max(length // 2, 1))
    fewer = place * (1 - right_half) + (length - 1 - place) * right_half

    def item(j):
        both_ways = at_least(2 * fewer, j + 1, 4 * length)
        step = both_ways * (j // 2) + (1 - both_ways) * (j - fewer)
        major = 1 - both_ways * (j % 2)
        rightward = major * (1 - right_half) + (1 - major) * right_half
        return rightward * (length - 1 - step) + (1 - rightward) * step, rightward

    items = [item(j) for j in range(length - 1)] + [(place, None)]
    pair_copies = {}

    def pair_sends(first, stop):
        for j in range(first, stop):
            home = items[j][0]
            if not direct:
                pair_up_out[j] = up_rows(2 * home + 1 - side, pl.ds(0, wide)).astype(BF16)
                pair_copies[0, j] = sends.start(
                    pair_up_out.at[j], pair_up_in.at[j], pair_sem.at[0, 0, j], pair_sem.at[1, 0, j], partner
                )
            pair_down_out[j] = down_rows(2 * home + 1 - side).astype(BF16)
            pair_copies[1, j] = sends.start(
                pair_down_out.at[j], pair_down_in.at[j], pair_sem.at[0, 1, j], pair_sem.at[1, 1, j], partner
            )

    has_left, has_right = at_least(place, 1, 2 * length), at_least(length - 1 - place, 1, 2 * length)
    inside = has_left * has_right

    def line_copy(kind, j, slot, device):
        if kind == 1:
            src, dst = line_down_out.at[j], line_down_in.at[slot]
        else:
            src, dst = line_up_out.at[j, :, columns[kind]], line_up_in.at[slot, :, columns[kind]]
        return pltpu.make_async_remote_copy(
            src_ref=src, dst_ref=dst, send_sem=line_sem.at[0, kind, j], recv_sem=line_sem.at[1, kind, slot],
            device_id=device, device_id_type=MESH,
        )

    def line_item(kind, j):
        home, rightward = items[j]
        if kind == 1:
            over, total, out, line_in = slice(None), down_ref, line_down_out, line_down_in
            pair_copies[1, j].wait_recv()
            total[...] = down_rows(2 * home + side) + pair_down_in[j].astype(F32)
        else:
            over, total, out, line_in = columns[kind], up_ref, line_up_out, line_up_in
            total[:, over] = up_pair(kind, j, home)
        if rightward is None:
            ways = [(has_left, place + 1), (has_right, place)]
        else:
            ways = [(rightward * has_left + (1 - rightward) * has_right, home + rightward)]
        for present, slot in ways:

            @pl.when(present == 1)
            def _():
                line_copy(kind, 0, slot, partner).wait_recv()
                total[:, over] += line_in[slot, :, over].astype(F32)

        if rightward is not None:
            out[j, :, over] = total[:, over].astype(BF16)
            line_copy(kind, j, home + rightward, {"ctx": block + 4 * rightward - 2}).start()

    def ends(*which, last=False):
        @pl.when(inside == 0)
        def _():
            for kind, j in which:
                if last or j < length - 1:
                    line_item(kind, j)

    def middles(*which, last=False):
        @pl.when(inside == 1)
        def _():
            for kind, j in which:
                if last or j < length - 1:
                    line_item(kind, j)

    base = (3 * blocks + block) * tokens

    def inverse_counts(start, shape):
        counts = base + start + 1 + lax.broadcasted_iota(jnp.int32, shape, 0)
        return 1.0 / counts.astype(F32)

    def ordered(i, first):
        if i:
            target_copies[i].wait_recv()
        targets = targets_ref[i, 0:1, :]
        chosen = jnp.concatenate([placing(flipped(me, j), targets).astype(BF16) for j in range(groups)], axis=0)
        found = jnp.concatenate(
            [slots_ref[j, (j ^ i) * capacity : ((j ^ i) + 1) * capacity, :] for j in range(groups)], axis=0
        )
        start = pl.multiple_of(flipped(me, i) * tokens_own, tokens_own)
        at = pl.ds(start, tokens_own)
        grads = contract_rows(chosen, found)
        scaled = (grads * inverse_counts(start, grads.shape)).astype(BF16)
        grad_ref[at, :] = grads.astype(BF16)
        scaled_grad_ref[at, :] = scaled
        for h in range(heads):
            cols = slice(h * head_dim, (h + 1) * head_dim)
            state = contract_rows(query_ref[at, cols], scaled[:, cols])
            local_ref[h] = state if first else state + local_ref[h]

    pair_sends(0, 1)
    for copy in other_copies:
        copy.wait_recv()
    ends((0, 0), (2, 0))
    pair_sends(1, length)
    project_near(2)
    ends((1, 0), (0, 1), (2, 1))
    middles((0, 0), (2, 0))
    project_far(0)
    ends((1, 1))
    middles((1, 0), (0, 1), (2, 1))
    project_far(1)
    middles((0, 2), (1, 1))
    for at in (5, 6, 7):
        loads[at].wait()
    ordered(2, True)
    ordered(3, False)
    project_far(2)
    ordered(0, False)
    ordered(1, False)

    some = heads // 2

    def state_copy(turn, at, device):
        return pltpu.make_async_remote_copy(
            src_ref=state_out_ref.at[turn % 3, at], dst_ref=state_in_ref.at[turn, at],
            send_sem=state_sem.at[0, turn, at], recv_sem=state_sem.at[1, turn, at],
            device_id=device, device_id_type=MESH,
        )

    line_ref[...] = jnp.zeros_like(line_ref)
    mine, theirs = side * some, (1 - side) * some
    for at in range(some):
        state_out_ref[0, at] = local_ref[theirs + at].astype(BF16)
        state_copy(0, at, partner).start()

    before_last = at_least(place, length - 2, 2 * length) * has_right
    left_block = lax.rem(block + blocks - 2, blocks)

    @pl.when((1 - has_right) * has_left == 1)
    def _():
        for at in range(some):
            state_out_ref[1, at] = local_ref[mine + at].astype(BF16)
            state_copy(1, at, {"ctx": left_block}).start()
            state_copy(3, at, {"ctx": lax.rem(left_block + 1 - 2 * side + blocks, blocks)}).start()

    def send_state(at):
        @pl.when(has_right * has_left == 1)
        def _():
            total = local_ref[mine + at] + state_in_ref[0, at].astype(F32)
            state_out_ref[1, at] = (total + line_ref[at]).astype(BF16)
            state_copy(1, at, {"ctx": left_block}).start()

    for j in range(2, length - 1):
        ends((0, j), (2, j), (1, j))
    middles((2, 2))

    own = jnp.concatenate([placing(flipped(me, j), own_target).astype(BF16) for j in range(groups)], axis=0)
    rows = jnp.concatenate([rows_ref[j, j * capacity : (j + 1) * capacity, :] for j in range(groups)], axis=0)
    resid_ref[...] = contract_rows(own, rows).astype(BF16)
    for k in range(1, groups):
        gate_copies[k].wait_recv()
    gates = None
    for k in range(groups):
        one = plain(gate_in_ref[k, :, :capacity], placing(flipped(me, k), own_target).astype(BF16))
        gates = one if gates is None else gates + one
    dgates_ref[...] = gates[0:1, :].astype(BF16)

    row = lax.broadcasted_iota(jnp.int32, (chunk, chunk), 0)
    col = lax.broadcasted_iota(jnp.int32, (chunk, chunk), 1)

    def forward(h, carry):
        cols = pl.ds(pl.multiple_of(h * head_dim, head_dim), head_dim)
        state = prior_ref[h]
        for at in range(tokens // chunk):
            rows = pl.ds(at * chunk, chunk)
            keys, values, grads = key_ref[rows, cols], value_ref[rows, cols], grad_ref[rows, cols]
            mix = jnp.where(col <= row, contract_cols(grads, values), 0.0).astype(BF16)
            out = plain(mix, keys) + contract_cols(grads, state.astype(BF16))
            dquery_ref[rows, cols] = (out * inverse_counts(at * chunk, out.shape)).astype(BF16)
            state = state + contract_rows(keys, values)
        return carry

    def backward(h, carry):
        cols = pl.ds(pl.multiple_of(h * head_dim, head_dim), head_dim)
        state = later_ref[h]
        for at in reversed(range(tokens // chunk)):
            rows = pl.ds(at * chunk, chunk)
            query, keys = query_ref[rows, cols], key_ref[rows, cols]
            values, scaled = value_ref[rows, cols], scaled_grad_ref[rows, cols]
            held = state.astype(BF16)
            mix_key = jnp.where(col >= row, contract_cols(values, scaled), 0.0).astype(BF16)
            dkey_ref[rows, cols] = (plain(mix_key, query) + contract_cols(values, held)).astype(BF16)
            mix_value = jnp.where(col >= row, contract_cols(keys, query), 0.0).astype(BF16)
            dvalue_ref[rows, cols] = (plain(mix_value, scaled) + plain(keys, held)).astype(BF16)
            state = state + contract_rows(query, scaled)
        return carry

    loads[8].wait()
    lax.fori_loop(0, heads, forward, 0)
    sends.drain()
    finals = [(0, length - 1), (2, length - 1), (1, length - 1)]
    ends(*finals, last=True)
    for at in range(some):
        state_copy(0, at, partner).wait_recv()

        @pl.when(has_right == 1)
        def _():
            state_copy(1, at, partner).wait_recv()
            line_ref[at] = state_in_ref[1, at].astype(F32)

        @pl.when(before_last == 1)
        def _():
            state_copy(3, at, partner).wait_recv()
            line_ref[at] += state_in_ref[3, at].astype(F32)

        send_state(at)
        state_out_ref[2, at] = (line_ref[at] + local_ref[mine + at] * side.astype(F32)).astype(BF16)
        state_copy(2, at, partner).start()
        later_ref[mine + at] = line_ref[at] + state_in_ref[0, at].astype(F32) * (1 - side).astype(F32)
    middles((1, 2))
    for j in range(3, length - 1):
        middles((0, j), (2, j), (1, j))
    lax.fori_loop(mine, mine + some, backward, 0)
    for at in range(some):
        state_copy(2, at, partner).wait_recv()
        later_ref[theirs + at] = state_in_ref[2, at].astype(F32)
    lax.fori_loop(theirs, theirs + some, backward, 0)
    middles(*finals, last=True)
    for kind in range(3):
        for j in range(length - 1):
            line_copy(kind, j, 0, partner).wait_send()

    for at in range(some):

        @pl.when(has_left == 1)
        def _():
            state_copy(1, at, partner).wait_send()

        @pl.when((1 - has_right) * has_left == 1)
        def _():
            state_copy(3, at, partner).wait_send()

        state_copy(0, at, partner).wait_send()
        state_copy(2, at, partner).wait_send()
    sends.drain()


def pass_kernel(count, *refs):
    sems, copies = refs[2 * count], []
    for at in range(count):
        rows = refs[at].shape[0]
        cuts = 2 if rows % 32 == 0 else 1
        for cut in range(cuts):
            part = pl.ds(cut * (rows // cuts), rows // cuts)
            copies.append(pltpu.make_async_copy(refs[at].at[part], refs[count + at].at[part], sems.at[at, cut]))
    for copy in copies:
        copy.start()
    for copy in copies:
        copy.wait()


def pass_on(*arrays):
    return pl.pallas_call(
        functools.partial(pass_kernel, len(arrays)),
        in_specs=[pl.BlockSpec(memory_space=pltpu.VMEM)] * len(arrays),
        out_specs=[pl.BlockSpec(memory_space=pl.ANY)] * len(arrays),
        out_shape=[jax.ShapeDtypeStruct(one.shape, one.dtype) for one in arrays],
        scratch_shapes=[pltpu.SemaphoreType.DMA((len(arrays), 2))],
        compiler_params=pltpu.CompilerParams(vmem_limit_bytes=1 << 20),
        name="pass_on",
    )(*[pltpu.with_memory_space_constraint(one, pltpu.VMEM) for one in arrays])


def compute(
    attn_query, attn_key, attn_value, prefix_state, moe_in, grad_out, router_gates, expert_ids,
    w_gate_up, w_down, w_out,
):
    groups, blocks = lax.axis_size("exp"), lax.axis_size("ctx")
    rows, width = moe_in.shape
    capacity = 3 * rows // (2 * groups * w_gate_up.shape[0])
    hidden_units, wide = w_down.shape[1], w_gate_up.shape[2]
    unit, unit_down = width // blocks, hidden_units // blocks
    tokens, cols = attn_query.shape
    heads, head_dim = prefix_state.shape[1:3]
    length = blocks // 2
    direct = unit % LANES == 0
    whole = pl.BlockSpec(memory_space=pltpu.VMEM)
    away = pl.BlockSpec(memory_space=pl.ANY)
    dma = pltpu.SemaphoreType.DMA
    vmem = pltpu.VMEM
    state = vmem((heads, head_dim, head_dim), F32)
    flat_ref = vmem((tokens, cols), BF16)
    scratch = [
        vmem((rows, width), BF16), vmem((rows, width), BF16),
        vmem((width, wide), BF16), vmem((hidden_units, width), BF16), vmem((cols, width), BF16),
        flat_ref, flat_ref, flat_ref, state, dma((9,)),
        vmem((groups, 8, rows), jnp.int32), dma((2, groups)),
        vmem((groups - 1, capacity, 2 * width), BF16), vmem((groups, capacity, 2 * width), BF16),
        vmem((groups - 1, 16, LANES), BF16), vmem((groups, 16, LANES), BF16), dma((2, groups, 4)),
        vmem((2, 2 * capacity, width), BF16), vmem((2, 2 * capacity, wide), BF16),
        vmem((2, hidden_units, 2 * capacity), BF16),
        vmem((groups - 1, 16, LANES), BF16), vmem((groups, 16, LANES), BF16), dma((2, groups)),
        vmem((groups, groups * capacity, width), BF16), dma((2, groups, 3)),
        vmem((groups, groups * capacity, cols), BF16),
        flat_ref, flat_ref,
        state, vmem((heads // 2, head_dim, head_dim), F32), state,
        vmem((3, heads // 2, head_dim, head_dim), BF16), vmem((4, heads // 2, head_dim, head_dim), BF16),
        dma((2, 4, heads // 2)),
        vmem((length, unit_down, width), BF16), vmem((length, unit_down, width), BF16), dma((2, 2, length)),
        vmem((length - 1, unit, wide), BF16), vmem((length + 1, unit, wide), BF16),
        vmem((length - 1, unit_down, width), BF16), vmem((length + 1, unit_down, width), BF16),
        dma((2, 3, length + 1)),
    ]
    if direct:
        scratch += [
            vmem((2, 2 * capacity, length * unit), BF16), vmem((2, 2 * capacity, wide), BF16),
            dma((2, groups * length + 4)),
        ]
    else:
        scratch += [
            vmem((2, width, 2 * capacity), BF16),
            vmem((length, unit, wide), BF16), vmem((length, unit, wide), BF16),
        ]
    found = pl.pallas_call(
        functools.partial(layer_kernel, groups, blocks, min(256, tokens), direct),
        in_specs=[whole] * 2 + [away] * 9,
        out_specs=[whole] * 7,
        out_shape=[
            flat_ref, flat_ref, flat_ref, vmem((rows, width), BF16), vmem((1, rows), BF16),
            vmem((unit, wide), F32), vmem((unit_down, width), F32),
        ],
        scratch_shapes=scratch,
        compiler_params=pltpu.CompilerParams(
            collective_id=0, has_side_effects=True, vmem_limit_bytes=56000000
        ),
        name="layer",
    )(
        expert_ids.reshape(1, rows), router_gates.reshape(1, rows), moe_in, grad_out, w_gate_up[0], w_down[0], w_out,
        attn_query, attn_key, attn_value, prefix_state[0],
    )
    dquery, dkey, dvalue, resid, dgates, up, down = pass_on(*found)
    return dquery, dkey, dvalue, resid, dgates.reshape(rows, 1), up, down


def on_device(*args):
    dquery, dkey, dvalue, resid, dgates, up, down = compute(*args)
    return dquery, dkey, dvalue, resid, dgates, up[None], down[None]


def solution(mesh):
    return jax.shard_map(
        on_device,
        mesh=mesh,
        in_specs=(
            P("ctx", "exp"),
            P("ctx", "exp"),
            P("ctx", "exp"),
            P("ctx", "exp", None, None),
            P(("ctx", "exp"), None),
            P(("ctx", "exp"), None),
            P(("ctx", "exp"), None),
            P(("ctx", "exp"), None),
            P("exp", None, None),
            P("exp", None, None),
            P("exp", None),
        ),
        out_specs=(
            P("ctx", "exp"),
            P("ctx", "exp"),
            P("ctx", "exp"),
            P(("ctx", "exp"), None),
            P(("ctx", "exp"), None),
            P("exp", "ctx", None),
            P("exp", "ctx", None),
        ),
        check_vma=False,
    )
```
